32 devices in a mesh: seq: 8 (over y, x, core), head: 4 (over z).
Axes of the slice: x: 2, y: 2, z: 4, core: 2. Of those that a mesh axis runs over, the one named last changes fastest.
Arguments:
- queries: bfloat16 [2048, 4096], P('seq', 'head'), may hold values from -40 to 40
- key_rows: bfloat16 [2048, 1024], P('seq', 'head'), may hold values from -10 to 10
- value_rows: bfloat16 [2048, 1024], P('seq', 'head'), may hold values from -6 to 6
- out_weight: bfloat16 [4096, 4096], P('head'), may hold values from -0.09375 to 0.09375
- ssm_input: bfloat16 [2048, 8192], P('seq', 'head'), may hold values from -6 to 6
- bc_input: bfloat16 [2048, 2, 1024], P('seq', None, 'head'), may hold values from -6 to 6
- conv_input: float32 [4, 8192], P(None, 'head'), may hold values from -3 to 3
- conv_bc: float32 [4, 2, 1024], P(None, None, 'head'), may hold values from -3 to 3
- step_size: float32 [2048, 128], P('seq', 'head'), may hold values from 0.01 to 0.1
- decay_rate: float32 [128], P('head'), may hold values from 1e-05 to 1
- skip_gain: float32 [128], P('head'), may hold values from 0.5 to 1.5
- doc_ids: int32 [2048], P('seq'), may hold values from 0 to 7, never falling along the last dimension, each value on 1 to 1024 neighbouring positions
Outputs:
- attn_out: bfloat16 [2048, 4096], P(('seq', 'head'))
- ssm_out: bfloat16 [2048, 8192], P('seq', 'head')
The draws below stay inside these ranges and needn't reach their ends.
Inputs may be any that keep to these rules, and one draw needn't show every extreme that they name: `doc_ids`: never falling along the sequence; each document covers at most 1024 positions and one covers exactly that many.
All inputs are finite; a program needn't handle non-finite values.
Results may differ from the reference program's by a relative error of at most 0.012.
Values may be sent and summed in bfloat16 or wider, within the bound.
No kernel may reach another device: no remote copies, remote signals or barrier semaphores. Data moves between devices by JAX's collectives and lax.ppermute only.
A program may use at most 192 MiB of HBM per device.

```python
import math
import jax
import jax.numpy as jnp
import numpy as np
from jax import lax

D = 4096
HEADS = 32
KV_HEADS = 8
HEAD_DIM = 128
SSM_HEADS = 128
SSM_DIM = 64
STATE = 128
GROUPS = 8
CONV = 4
SB = 128
ROWS_DEV = 256
SHARDS = 8
TOKENS = 2048


def drawn_pair(key):
    query_key = jax.random.fold_in(key, 101)
    key_key = jax.random.fold_in(key, 202)
    query_draw = jax.random.truncated_normal(query_key, -4.0, 4.0, (TOKENS, HEADS * HEAD_DIM), jnp.float32)
    key_draw = jax.random.truncated_normal(key_key, -4.0, 4.0, (TOKENS, KV_HEADS * HEAD_DIM), jnp.float32)
    return (query_draw, key_draw)


def draw_queries(key, part):
    return drawn_pair(key)[0].astype(jnp.bfloat16)


def draw_key_rows(key, part):
    return drawn_pair(key)[1].astype(jnp.bfloat16)


def levels(stream_key, extent, split, smallest, largest):
    loudness, own = 1.0, jax.random.fold_in(stream_key, 6)
    for dim, parts in split:
        draws = jnp.exp(jax.random.uniform(jax.random.fold_in(own, dim), (parts,), jnp.float32, smallest / len(split), largest / len(split)))
        loudness = loudness * jnp.repeat(draws, extent[dim] // parts).reshape([-1 if axis == dim else 1 for axis in range(len(extent))])
    return loudness


def split_up(number_of, total, reach, slope):
    portions = [(1 << 20) // math.isqrt(rank ** slope) + 1 for rank in range(2, number_of + 1)]
    rest, holding = total - reach - (number_of - 1), [1] * (number_of - 1)
    while rest > 0:
        candidates = [i for i in range(number_of - 1) if holding[i] < reach]
        whole, remaining = sum([portions[i] for i in candidates]), rest
        for i in candidates:
            more = min(reach - holding[i], max(1, remaining * portions[i] // whole), rest)
            holding[i] = holding[i] + more
            rest = rest - more
    return np.array([reach] + holding)


def ragged_sizes(rng, count, total, most, lean):
    if count == 2:
        one = jax.random.randint(rng, (), max(1, total - most), min(most, total - 1) + 1)
        return jnp.stack([one, total - one])
    sizes = jnp.asarray(split_up(count, total, most, lean), jnp.int32)
    pairs = (count - 1) // 2
    giver, taker = sizes[1:1 + 2 * pairs:2], sizes[2:2 + 2 * pairs:2]
    room = jnp.minimum(giver - 1, most - taker)
    passed = jax.random.randint(jax.random.fold_in(rng, 1), (pairs,), 0, 1 << 20) % (room + 1)
    sizes = sizes.at[1:1 + 2 * pairs:2].set(giver - passed).at[2:2 + 2 * pairs:2].set(taker + passed)
    return sizes[jax.random.permutation(jax.random.fold_in(rng, 2), count)]


def bell_draw(own_key, dims, deviation, limit, shards=(), kind=jnp.bfloat16):
    array = deviation * jax.random.normal(own_key, dims, jnp.float32)
    if shards:
        array = array * levels(own_key, dims, shards, -0.22, 0.18)
    return jnp.clip(array, -limit, limit).astype(kind)


def setup_inputs(seed: int = 0) -> dict:
    key_list = jax.random.split(jax.random.key(seed), 13)
    return {
        "queries": draw_queries(jax.random.fold_in(key_list[12], 71), 0),
        "key_rows": draw_key_rows(jax.random.fold_in(key_list[12], 71), 0),
        "value_rows": bell_draw(key_list[2], (TOKENS, KV_HEADS * HEAD_DIM), 1.0, 6.0, ((0, 8), (1, 4))),
        "out_weight": bell_draw(key_list[3], (HEADS * HEAD_DIM, D), (HEADS * HEAD_DIM) ** -0.5, 0.09375, ((0, 4),)),
        "ssm_input": bell_draw(key_list[4], (TOKENS, SSM_HEADS * SSM_DIM), 1.0, 6.0, ((0, 8), (1, 4))),
        "bc_input": bell_draw(key_list[5], (TOKENS, 2, GROUPS * STATE), 1.0, 6.0, ((0, 8), (2, 4))),
        "conv_input": bell_draw(key_list[6], (CONV, SSM_HEADS * SSM_DIM), CONV ** -0.5, 3.0, ((1, 4),), jnp.float32),
        "conv_bc": bell_draw(key_list[7], (CONV, 2, GROUPS * STATE), CONV ** -0.5, 3.0, ((2, 4),), jnp.float32),
        "step_size": jnp.clip(jnp.exp(math.log(0.1) - 2.3025851 * jax.random.uniform(key_list[8], (TOKENS, SSM_HEADS), jnp.float32) ** levels(key_list[8], (TOKENS, SSM_HEADS), ((0, 8), (1, 4)), -0.2, 0.2)), 0.01, 0.1),
        "decay_rate": jnp.clip(jnp.exp(math.log(1.0) - 11.512925 * jax.random.uniform(key_list[9], (SSM_HEADS,), jnp.float32) ** levels(key_list[9], (SSM_HEADS,), ((0, 4),), -0.2, 0.2)), 9.999999747378752e-06, 1.0),
        "skip_gain": jnp.clip(0.5 + 1.0 * jax.random.uniform(key_list[10], (SSM_HEADS,), jnp.float32) ** levels(key_list[10], (SSM_HEADS,), ((0, 4),), -0.2, 0.2), 0.5, 1.5),
        "doc_ids": jnp.searchsorted(jnp.cumsum(ragged_sizes(key_list[11], TOKENS // ROWS_DEV, TOKENS, TOKENS // 2, 2)), jnp.arange(TOKENS), side="right").astype(jnp.int32),
    }


NEG_BIG = -1e+30

def row_positions(total_rows, rows_dev, shard_count):
    row_ids = jnp.arange(total_rows, dtype=jnp.int32)
    half_rows = rows_dev // 2
    device = row_ids // rows_dev
    within = row_ids % rows_dev
    block_id = jnp.where(within < half_rows, device, 2 * shard_count - 1 - device)
    return block_id * half_rows + within % half_rows

def layout_rows(total_rows, rows_dev, shard_count):
    places = jnp.arange(total_rows, dtype=jnp.int32)
    half_rows = rows_dev // 2
    block_id = places // half_rows
    device = jnp.where(block_id < shard_count, block_id, 2 * shard_count - 1 - block_id)
    offset = jnp.where(block_id < shard_count, 0, half_rows)
    return (device * rows_dev + offset + places % half_rows).astype(jnp.int32)

def attention_seq(query_seq, key_seq, value_seq, doc_ids):
    total_rows = query_seq.shape[0]
    group_size = HEADS // KV_HEADS
    block_count = total_rows // ROWS_DEV
    query_blocks = query_seq.reshape(block_count, ROWS_DEV, KV_HEADS, group_size, HEAD_DIM)
    query_places = jnp.arange(total_rows, dtype=jnp.int32).reshape(block_count, ROWS_DEV)
    key_heads = jnp.transpose(key_seq.reshape(total_rows, KV_HEADS, HEAD_DIM).astype(jnp.float32), (1, 0, 2))
    value_heads = jnp.transpose(value_seq.reshape(total_rows, KV_HEADS, HEAD_DIM).astype(jnp.float32), (1, 0, 2))
    places = jnp.arange(total_rows, dtype=jnp.int32)
    attention_score_scale = 1.0 / math.sqrt(HEAD_DIM)

    def one_block(block_args):
        query_block, query_place = block_args
        query_doc = doc_ids[query_place]
        allowed = (places[None, :] <= query_place[:, None]) & (doc_ids[None, :] == query_doc[:, None])

        def one_head(head_args):
            head_query_rows, head_key_rows, head_value_rows = head_args
            logit_scores = jnp.einsum('suj,yj->usy', head_query_rows.astype(jnp.float32), head_key_rows) * attention_score_scale
            masked = jnp.where(allowed[None], logit_scores, NEG_BIG)
            row_top = lax.optimization_barrier(jnp.max(masked, axis=-1, keepdims=True))
            weights = jnp.where(allowed[None], jnp.exp(masked - row_top), 0.0)
            weight_sum = lax.optimization_barrier(jnp.sum(weights, axis=-1))
            rounded_values = lax.optimization_barrier(weights.astype(jnp.bfloat16)).astype(jnp.float32)
            mixture_total_sum = jnp.einsum('vnw,wm->vnm', rounded_values, head_value_rows)
            return (mixture_total_sum / weight_sum[..., None]).astype(jnp.bfloat16)
        outputs = lax.map(one_head, (jnp.transpose(query_block, (1, 0, 2, 3)), key_heads, value_heads))
        return jnp.transpose(outputs, (2, 0, 1, 3)).reshape(ROWS_DEV, HEADS * HEAD_DIM)
    context = lax.map(one_block, (query_blocks, query_places))
    return context.reshape(total_rows, HEADS * HEAD_DIM)

def conv_seq(input_seq, taps, doc_ids):
    total_rows = input_seq.shape[0]
    input_float = input_seq.astype(jnp.float32)
    accum = jnp.zeros(input_float.shape, jnp.float32)
    for tap_index in range(CONV):
        shifted = jnp.pad(input_float, ((tap_index, 0), (0, 0)))[:total_rows]
        doc_shift = jnp.pad(doc_ids, (tap_index, 0), constant_values=-1)[:total_rows]
        keep_rows = (doc_shift == doc_ids)[:, None]
        accum = accum + jnp.where(keep_rows, taps[tap_index][None, :] * shifted, 0.0)
    return jax.nn.silu(accum).astype(jnp.bfloat16)

def ssd_block(block_carry, block_part, head_rates):
    state_in, last_doc = block_carry
    x_block, b_block, c_block, step_block, doc_block = block_part
    block_rows = x_block.shape[0]
    log_decay = jnp.cumsum(-head_rates[None] * step_block, axis=0)
    log_rows = jnp.transpose(log_decay, (1, 2, 0))
    row_ids = jnp.arange(block_rows)
    same_doc = (doc_block[:, None] == doc_block[None, :]) & (row_ids[:, None] >= row_ids[None, :])
    logit_scores = jnp.einsum('tgn,sgn->gts', c_block.astype(jnp.float32), b_block.astype(jnp.float32))
    log_gap = jnp.where(same_doc, log_rows[..., :, None] - log_rows[..., None, :], 0.0)
    step_cols = jnp.transpose(step_block, (1, 2, 0))
    weights = jnp.where(same_doc, logit_scores[:, None] * jnp.exp(log_gap) * step_cols[..., None, :], 0.0)
    rounded_values = lax.optimization_barrier(weights.astype(jnp.bfloat16)).astype(jnp.float32)
    inner_sum = jnp.einsum('gets,sgep->tgep', rounded_values, x_block.astype(jnp.float32))
    alive_rows = (doc_block == last_doc).astype(jnp.float32)
    reach_rows = jnp.exp(log_decay) * alive_rows[:, None, None]
    carried = jnp.einsum('tgn,gepn->tgep', c_block.astype(jnp.float32), state_in, precision=lax.Precision.HIGHEST)
    block_out = inner_sum + reach_rows[..., None] * carried
    end_doc = doc_block[block_rows - 1]
    keep_rows = (doc_block == end_doc).astype(jnp.float32)
    log_end = log_decay[block_rows - 1]
    fade_rows = jnp.exp(log_end[None] - log_decay) * step_block * keep_rows[:, None, None]
    scaled = lax.optimization_barrier((fade_rows[..., None] * x_block.astype(jnp.float32)).astype(jnp.bfloat16))
    fresh_state = jnp.einsum('sgep,sgn->gepn', scaled.astype(jnp.float32), b_block.astype(jnp.float32))
    keep_state = jnp.exp(log_end) * (end_doc == last_doc).astype(jnp.float32)
    new_state = keep_state[..., None, None] * state_in + fresh_state
    return ((new_state, end_doc), block_out)

def ssd_seq(x_conv, bc_conv, step_seq, decay_rate, doc_ids):
    total_rows = x_conv.shape[0]
    block_count = total_rows // SB
    per_group = SSM_HEADS // GROUPS
    x_blocks = x_conv.reshape(block_count, SB, GROUPS, per_group, SSM_DIM)
    b_blocks = bc_conv[:, 0].reshape(block_count, SB, GROUPS, STATE)
    c_blocks = bc_conv[:, 1].reshape(block_count, SB, GROUPS, STATE)
    step_blocks = step_seq.reshape(block_count, SB, GROUPS, per_group)
    doc_blocks = doc_ids.reshape(block_count, SB)
    head_rates = decay_rate.reshape(GROUPS, per_group)
    start_carry = (jnp.zeros((GROUPS, per_group, SSM_DIM, STATE), jnp.float32), jnp.int32(-1))

    def block_step(block_carry, block_part):
        return ssd_block(block_carry, block_part, head_rates)
    final_carry, outputs = lax.scan(block_step, start_carry, (x_blocks, b_blocks, c_blocks, step_blocks, doc_blocks))
    return outputs.reshape(total_rows, GROUPS, per_group, SSM_DIM)

def reference(queries, key_rows, value_rows, out_weight, ssm_input, bc_input, conv_input, conv_bc, step_size, decay_rate, skip_gain, doc_ids):
    total_rows = queries.shape[0]
    to_layout = row_positions(total_rows, ROWS_DEV, SHARDS)
    from_layout = layout_rows(total_rows, ROWS_DEV, SHARDS)
    context = attention_seq(queries[from_layout], key_rows[from_layout], value_rows[from_layout], doc_ids)
    context_layout = context[to_layout]
    attn_out = jnp.dot(context_layout, out_weight, preferred_element_type=jnp.float32).astype(jnp.bfloat16)
    x_conv = conv_seq(ssm_input[from_layout], conv_input, doc_ids)
    bc_seq = bc_input[from_layout].reshape(total_rows, 2 * GROUPS * STATE)
    bc_conv = conv_seq(bc_seq, conv_bc.reshape(CONV, 2 * GROUPS * STATE), doc_ids).reshape(total_rows, 2, GROUPS * STATE)
    per_group = SSM_HEADS // GROUPS
    mixed_seq = ssd_seq(x_conv, bc_conv, step_size[from_layout], decay_rate, doc_ids)
    x_float = x_conv.astype(jnp.float32).reshape(total_rows, GROUPS, per_group, SSM_DIM)
    mixed_seq = mixed_seq + skip_gain.reshape(GROUPS, per_group)[None, :, :, None] * x_float
    ssm_seq = mixed_seq.reshape(total_rows, SSM_HEADS * SSM_DIM).astype(jnp.bfloat16)
    return (attn_out, ssm_seq[to_layout])
```

```python
import functools
import math

import jax
import jax.numpy as jnp
from jax import lax
from jax.experimental import pallas as pl
from jax.experimental.pallas import tpu as pltpu
from jax.sharding import PartitionSpec as P

HEAD_DIM = 128
STATE = 128
SB = 128
LEAD = 8

NEG_BIG = -1e30
BF = jnp.bfloat16
F32 = jnp.float32
HI = lax.Precision.HIGHEST


def anywhere():
    return pl.BlockSpec(memory_space=pl.ANY)


def vmem():
    return pl.BlockSpec(memory_space=pltpu.VMEM)


def smem():
    return pl.BlockSpec(memory_space=pltpu.SMEM)


def swap(x, bit):
    count = lax.axis_size("seq")
    return lax.ppermute(x, "seq", [(i, i ^ bit) for i in range(count)])


def chip_bits(count):
    bits, bit = [], 2
    while bit < count:
        bits.append(bit)
        bit *= 2
    return bits


def two_way_gather(front, back, whole):
    count = lax.axis_size("seq")
    bits = chip_bits(count)
    pieces = [(0, None, whole)]
    fronts, backs = {0: front}, {0: back}
    for bit in bits:
        got = swap(whole, bit)
        pieces.append((bit, None, got))
        half_rows = got.shape[0] // 2
        fronts[bit], backs[bit] = got[:half_rows], got[half_rows:]
    for pattern in range(2, count, 2):
        if pattern in bits:
            continue
        high = max(bit for bit in bits if pattern & bit)
        low = min(bit for bit in bits if pattern & bit)
        fronts[pattern] = swap(fronts[pattern ^ high], high)
        pieces.append((pattern, 0, fronts[pattern]))
    for pattern in range(2, count, 2):
        if pattern in bits:
            continue
        low = min(bit for bit in bits if pattern & bit)
        backs[pattern] = swap(backs[pattern ^ low], low)
        pieces.append((pattern, 1, backs[pattern]))
    return pieces


def attend_kernel(
    places, half, count, is_back, ids_ref, docs_ref, docs_s, q_ref, w_ref, *rest
):
    total = len(places)
    pieces = rest[:total]
    send_ref, keep_ref, kvs, ws, scores, top, acc, ctx, kv_sem, w_sem = rest[total:]
    me = ids_ref[0]
    odd = ids_ref[1]
    rows = q_ref.shape[0]
    width = pieces[0].shape[-1]
    kv_heads = width // (2 * HEAD_DIM)
    group = q_ref.shape[1] // (kv_heads * HEAD_DIM)
    w_copy = pltpu.make_async_copy(w_ref, ws, w_sem)
    w_copy.start()
    copies = []
    for at, (pattern, part) in enumerate(places):
        owner = lax.bitwise_xor(me, pattern)
        if part is None:
            halves = ((0, 0, rows), (1, rows, rows)) if is_back else ((0, 0, rows),)
        else:
            halves = ((part, 0, rows),) if (part == 0 or is_back) else ()
        for which, first, size in halves:
            block = owner if which == 0 else 2 * count - 1 - owner
            copy = pltpu.make_async_copy(
                pieces[at].at[pl.ds(first, size)],
                kvs.at[pl.ds(pl.multiple_of(block * rows, rows), rows)],
                kv_sem.at[len(copies)],
            )
            copy.start()
            copies.append(copy)
    block = 2 * count - 1 - me if is_back else me

    def doc_at(where, lane):
        slot = lax.bitwise_xor(lax.shift_right_logical(where, 1), me)
        return docs_s[slot, lax.rem(where, 2) * rows + lane]

    first_doc = doc_at(block, 0)

    def count_step(at, skipped):
        return skipped + jnp.where(doc_at(at, rows - 1) < first_doc, 1, 0)

    start = lax.fori_loop(0, block, count_step, 0)
    tile_rows = 2 * rows
    first_tile = lax.shift_right_logical(start, 1)
    last_tile = lax.shift_right_logical(block, 1) + 1
    own = docs_ref[pl.ds(lax.bitwise_xor(lax.shift_right_logical(block, 1), me), 1), :]
    own = jnp.where(lax.rem(block, 2) == 1, own[:, rows:], own[:, :rows])
    own_col = jnp.transpose(jnp.broadcast_to(own, (rows, rows)))[:, :1]
    q_place = block * rows + lax.broadcasted_iota(jnp.int32, (rows, tile_rows), 0)
    k_place = lax.broadcasted_iota(jnp.int32, (rows, tile_rows), 1)
    for copy in copies:
        copy.wait()
    scale = math.log2(math.e) / math.sqrt(HEAD_DIM)
    for kv in range(kv_heads):
        heads = [kv * group + e for e in range(group)]
        q = jnp.concatenate(
            [q_ref[:, h * HEAD_DIM : (h + 1) * HEAD_DIM] for h in heads], axis=0
        )
        top[...] = jnp.full(top.shape, NEG_BIG, F32)
        acc[...] = jnp.zeros(acc.shape, F32)

        def score_step(tile, carry, q=q, kv=kv):
            at = pl.multiple_of(tile * tile_rows, tile_rows)
            keys = kvs[pl.ds(at, tile_rows), kv * HEAD_DIM : (kv + 1) * HEAD_DIM]
            docs = docs_ref[pl.ds(lax.bitwise_xor(tile, me), 1), :]
            allowed = (k_place + at <= q_place) & (docs == own_col)
            found = lax.dot_general(q, keys, (((1,), (1,)), ((), ())), preferred_element_type=F32)
            found = jnp.where(
                allowed[None], found.reshape(group, rows, tile_rows), NEG_BIG
            ).reshape(group * rows, tile_rows)
            scores[tile] = found
            top[...] = jnp.maximum(
                top[...], jnp.maximum(found[:, :HEAD_DIM], found[:, HEAD_DIM:])
            )
            return carry

        lax.fori_loop(first_tile, last_tile, score_step, 0)
        row_top = jnp.max(top[...], axis=1, keepdims=True)

        def mix_step(tile, carry, row_top=row_top, kv=kv):
            at = pl.multiple_of(tile * tile_rows, tile_rows)
            first = (kv_heads + kv) * HEAD_DIM
            values = kvs[pl.ds(at, tile_rows), first : first + HEAD_DIM]
            values = jnp.concatenate([values, jnp.ones_like(values)], axis=1)
            weights = jnp.exp2((scores[tile] - row_top) * scale).astype(BF)
            acc[...] += jnp.dot(weights, values, preferred_element_type=F32)
            return carry

        lax.fori_loop(first_tile, last_tile, mix_step, 0)
        mixed = (acc[:, :HEAD_DIM] / acc[:, HEAD_DIM:]).astype(BF)
        for e, h in enumerate(heads):
            ctx[:, h * HEAD_DIM : (h + 1) * HEAD_DIM] = mixed[e * rows : (e + 1) * rows]
    w_copy.wait()
    part_rows = rows // 2

    def project(at, carry):
        lanes = pl.ds(pl.multiple_of(at * 512, 512), 512)
        made = jnp.dot(ctx[...], ws[:, lanes], preferred_element_type=F32).astype(BF)
        lower, upper = made[:part_rows], made[part_rows:]

        @pl.when(odd == 0)
        def _():
            keep_ref[:, lanes] = lower
            send_ref[:, lanes] = upper

        @pl.when(odd == 1)
        def _():
            keep_ref[:, lanes] = upper
            send_ref[:, lanes] = lower

        return carry

    lax.fori_loop(0, w_ref.shape[1] // 512, project, 0)


def attend(ids, docs, queries, out_weight, pieces, is_back):
    count = docs.shape[0]
    rows = queries.shape[0] // 2
    places = [(pattern, part) for pattern, part, _ in pieces]
    arrays = [array for _, _, array in pieces]
    kv_width = arrays[0].shape[1]
    kv_heads = kv_width // (2 * HEAD_DIM)
    group = queries.shape[1] // (kv_heads * HEAD_DIM)
    features, columns = out_weight.shape
    half = 1 if is_back else 0
    return pl.pallas_call(
        functools.partial(attend_kernel, places, half, count, is_back),
        grid=(1,),
        in_specs=[
            smem(),
            vmem(),
            smem(),
            pl.BlockSpec((rows, queries.shape[1]), lambda t: (half, 0)),
            anywhere(),
        ]
        + [anywhere()] * len(arrays),
        out_specs=[vmem(), vmem()],
        out_shape=[jax.ShapeDtypeStruct((rows // 2, columns), BF)] * 2,
        scratch_shapes=[
            pltpu.VMEM((2 * count * rows, kv_width), BF),
            pltpu.VMEM((features, columns), BF),
            pltpu.VMEM((count, group * rows, 2 * rows), F32),
            pltpu.VMEM((group * rows, HEAD_DIM), F32),
            pltpu.VMEM((group * rows, 2 * HEAD_DIM), F32),
            pltpu.VMEM((rows, queries.shape[1]), BF),
            pltpu.SemaphoreType.DMA((2 * count,)),
            pltpu.SemaphoreType.DMA,
        ],
        cost_estimate=pl.CostEstimate(
            flops=2 * rows * features * columns, bytes_accessed=12 << 20, transcendentals=rows * 8192
        ),
        name="attend_back" if is_back else "attend_front",
    )(ids, docs, docs, queries, out_weight, *arrays)


def spread(values, expand):
    high = values.astype(BF)
    low = (values - high.astype(F32)).astype(BF)
    return jnp.dot(jnp.concatenate([high, low], axis=1), expand, preferred_element_type=F32)


def local_kernel(
    count, ids_ref, docs_ref, x_ref, bc_ref, lead_ref, tx_ref, tbc_ref, step_ref, rate_ref, expand_ref,
    xc_ref, xt_ref, mix_ref, reach_ref, keep_ref, send_ref, ext,
):
    half = pl.program_id(0)
    me = ids_ref[0]
    core = lax.rem(me, 2)
    rows, x_width = x_ref.shape
    bc_width = bc_ref.shape[1]
    groups = bc_width // (2 * STATE)
    x_group = x_width // groups
    block = jnp.where(half == 0, me, 2 * count - 1 - me)

    def doc_row(where):
        slot = lax.bitwise_xor(lax.shift_right_logical(where, 1), me)
        got = docs_ref[pl.ds(slot, 1), :]
        return jnp.where(lax.rem(where, 2) == 1, got[:, rows:], got[:, :rows])

    own = doc_row(block)
    before = jnp.where(block > 0, doc_row(jnp.maximum(block - 1, 0)), -1)
    lane = lax.broadcasted_iota(jnp.int32, (1, rows), 1)
    own_b = jnp.broadcast_to(own, (8, rows))
    before_b = jnp.broadcast_to(before, (8, rows))
    lane_b = jnp.broadcast_to(lane, (8, rows))
    lines = []
    for k in range(1, 4):
        moved = jnp.where(lane_b < k, pltpu.roll(before_b, k, 1), pltpu.roll(own_b, k, 1))
        lines.append((moved == own_b)[:1].astype(F32))
    last_doc = before[:, rows - 1 :]
    end_doc = own[:, rows - 1 :]
    lines.append((own == end_doc).astype(F32))
    lines.append((own == last_doc).astype(F32))
    lines.append(own.astype(F32))
    lines.append(jnp.zeros((2, rows), F32))
    table = jnp.transpose(jnp.concatenate(lines, axis=0))
    same = [table[:, k : k + 1] for k in range(3)]
    ending, alive, own_col = table[:, 3:4], table[:, 4:5], table[:, 5:6]

    def conv(source, taps, lead, width):
        ext[:LEAD, :width] = lead.astype(F32)
        ext[LEAD:, :width] = source.astype(F32)
        total = ext[LEAD:, :width] * taps[0:1]
        for k in range(1, 4):
            total += same[k - 1] * (ext[LEAD - k : LEAD - k + rows, :width] * taps[k : k + 1])
        return (total * (0.5 * jnp.tanh(0.5 * total) + 0.5)).astype(BF)

    bc = conv(bc_ref[...], tbc_ref[...], lead_ref[0, :, x_width:], bc_width)
    row_id = lax.broadcasted_iota(jnp.int32, (rows, rows), 0)
    col_id = lax.broadcasted_iota(jnp.int32, (rows, rows), 1)
    lower = row_id >= col_id
    steps = step_ref[...]
    logs = jnp.dot(
        lower.astype(F32), -rate_ref[...] * steps, preferred_element_type=F32, precision=HI
    )
    grow = jnp.exp(-logs) * steps
    reach = jnp.exp(logs)
    reach_ref[...] = reach
    expand = expand_ref[...]
    fade_end = spread(reach[rows - 8 :], expand)[7:8]
    carries = jnp.max(jnp.where(end_doc == last_doc, 1.0, 0.0))
    fade = fade_end * carries
    fade_high = fade.astype(BF)
    fade_low = (fade - fade_high.astype(F32)).astype(BF)
    allowed = lower & (own_col == own.astype(F32))
    for g in range(groups):
        lanes = slice(g * x_group, (g + 1) * x_group)
        xc = conv(x_ref[:, lanes], tx_ref[:, lanes], lead_ref[0, :, lanes], x_group)
        xc_ref[:, lanes] = xc
        xt = (xc.astype(F32) * spread(grow, expand[:, lanes])).astype(BF)
        xt_ref[:, lanes] = xt
        b = bc[:, g * STATE : (g + 1) * STATE]
        c = bc[:, (groups + g) * STATE : (groups + g + 1) * STATE]
        cb = lax.dot_general(c, b, (((1,), (1,)), ((), ())), preferred_element_type=F32)
        mix_ref[:, g * 2 * rows : g * 2 * rows + rows] = jnp.where(allowed, cb, 0.0).astype(BF)
        mix_ref[:, g * 2 * rows + rows : (g + 1) * 2 * rows] = (c.astype(F32) * alive).astype(BF)
        b_t = jnp.transpose(b.astype(F32) * ending).astype(BF)
        state = jnp.dot(b_t, xt, preferred_element_type=F32) * fade_end[:, lanes]
        packed = jnp.concatenate(
            [
                state.astype(BF),
                jnp.broadcast_to(fade_high[:, lanes], (8, x_group)),
                jnp.broadcast_to(fade_low[:, lanes], (8, x_group)),
            ],
            axis=0,
        )

        @pl.when(core == g)
        def _(packed=packed):
            keep_ref[0] = packed

        @pl.when(core != g)
        def _(packed=packed):
            send_ref[0] = packed


def unpack(packed):
    state = packed[:STATE].astype(F32)
    fade = packed[STATE : STATE + 1].astype(F32) + packed[STATE + 8 : STATE + 9].astype(F32)
    return fade, state


def pack(fade, state):
    high = fade.astype(BF)
    low = (fade - high.astype(F32)).astype(BF)
    shape = (8, state.shape[1])
    return jnp.concatenate(
        [state.astype(BF), jnp.broadcast_to(high, shape), jnp.broadcast_to(low, shape)], axis=0
    )


def join_kernel(ids_ref, mine_ref, other_ref, out_ref):
    core = lax.rem(ids_ref[0], 2)
    for half in range(2):
        first_is_mine = core == half

        def joined(first, second):
            fade_a, state_a = unpack(first)
            fade_b, state_b = unpack(second)
            return pack(fade_a * fade_b, fade_b * state_a + state_b)

        @pl.when(first_is_mine)
        def _(half=half):
            out_ref[half] = joined(mine_ref[half], other_ref[half])

        @pl.when(jnp.logical_not(first_is_mine))
        def _(half=half):
            out_ref[half] = joined(other_ref[half], mine_ref[half])


def enter_kernel(places, count, ids_ref, mine_ref, other_ref, *rest):
    total = len(places)
    pieces = rest[:total]
    keep_ref, send_ref, fronts, backs, sems, run = rest[total:]
    me = ids_ref[0]
    core = lax.rem(me, 2)
    chip = lax.shift_right_logical(me, 1)
    chips = count // 2
    copies = []
    for at, (pattern, part) in enumerate(places):
        slot = lax.bitwise_xor(chip, pattern // 2)
        for which in (0, 1) if part is None else (part,):
            source = pieces[at].at[which if part is None else 0]
            target = (fronts if which == 0 else backs).at[slot]
            copy = pltpu.make_async_copy(source, target, sems.at[len(copies)])
            copy.start()
            copies.append(copy)
    for copy in copies:
        copy.wait()
    run[...] = jnp.zeros(run.shape, F32)

    def put(half):
        entering = run[...]
        mine_first = core == half

        def after(packed):
            fade, state = unpack(packed)
            return (fade * entering + state).astype(BF)

        @pl.when(mine_first)
        def _():
            keep_ref[half] = entering.astype(BF)
            send_ref[half] = after(mine_ref[half])

        @pl.when(jnp.logical_not(mine_first))
        def _():
            send_ref[half] = entering.astype(BF)
            keep_ref[half] = after(other_ref[half])

    def front_step(at, carry):
        @pl.when(at == chip)
        def _():
            put(0)

        fade, state = unpack(fronts[at])
        run[...] = fade * run[...] + state
        return carry

    lax.fori_loop(0, chips, front_step, 0)

    def back_step(k, carry):
        at = chips - 1 - k

        @pl.when(at == chip)
        def _():
            put(1)

        fade, state = unpack(backs[at])
        run[...] = fade * run[...] + state
        return carry

    lax.fori_loop(0, chips - chip, back_step, 0)


def finish_kernel(
    ids_ref, xc_ref, xt_ref, mix_ref, reach_ref, skip_ref, expand_ref, mine_ref, other_ref, out_ref, both
):
    core = lax.rem(ids_ref[0], 2)
    rows, x_width = xc_ref.shape
    groups = mix_ref.shape[1] // (2 * rows)
    x_group = x_width // groups
    for g in range(groups):
        lanes = slice(g * x_group, (g + 1) * x_group)
        expand = expand_ref[:, lanes]
        both[:rows] = xt_ref[:, lanes]

        @pl.when(core == g)
        def _():
            both[rows:] = mine_ref[0]

        @pl.when(core != g)
        def _():
            both[rows:] = other_ref[0]

        mix = mix_ref[:, g * 2 * rows : (g + 1) * 2 * rows]
        made = jnp.dot(mix, both[...], preferred_element_type=F32)
        made = made * spread(reach_ref[...], expand)
        skip = spread(skip_ref[...], expand)[:1]
        out_ref[:, lanes] = (made + skip * xc_ref[:, lanes].astype(F32)).astype(BF)


def shards(
    queries, key_rows, value_rows, out_weight, ssm_input, bc_input, conv_input, conv_bc, step_size,
    decay_rate, skip_gain, doc_ids,
):
    count = lax.axis_size("seq")
    me = lax.axis_index("seq")
    z = lax.axis_index("head")
    rows_dev = queries.shape[0]
    rows = rows_dev // 2
    ids = jnp.stack([me, lax.rem(z, 2)]).astype(jnp.int32)

    docs = doc_ids.reshape(1, rows_dev)
    bit = 1
    while bit < count:
        docs = jnp.concatenate([docs, swap(docs, bit)], axis=0)
        bit *= 2

    x_width = ssm_input.shape[1]
    bc = bc_input.reshape(rows_dev, -1)
    bc_width = bc.shape[1]
    taps = conv_input.shape[0]
    edge_front = jnp.concatenate([ssm_input[rows - LEAD : rows], bc[rows - LEAD : rows]], axis=1)
    edge_back = jnp.concatenate([ssm_input[rows_dev - LEAD :], bc[rows_dev - LEAD :]], axis=1)
    lead_front = lax.ppermute(edge_front, "seq", [(i, i + 1) for i in range(count - 1)])
    lead_back = lax.ppermute(edge_back, "seq", [(i + 1, i) for i in range(count - 1)])
    lead_back = jnp.where(me == count - 1, edge_front, lead_back)
    lead = jnp.stack([lead_front, lead_back])

    kv = jnp.concatenate([key_rows, value_rows], axis=1)
    pieces = two_way_gather(kv[:rows], kv[rows:], kv)
    pieces = pieces + [(pattern ^ 1, part, swap(array, 1)) for pattern, part, array in pieces]

    groups = bc_width // (2 * STATE)
    heads = decay_rate.shape[0]
    x_group = x_width // groups
    expand = jnp.repeat(jnp.eye(heads, dtype=BF), x_width // heads, axis=1)
    expand = jnp.concatenate([expand, expand], axis=0)
    pack_rows = STATE + 16
    full = lambda shape: pl.BlockSpec(shape, lambda h: (0,) * len(shape))
    half = lambda width: pl.BlockSpec((rows, width), lambda h: (h, 0))
    packed_spec = pl.BlockSpec((1, pack_rows, x_group), lambda h: (h, 0, 0))
    xc, xt, mix, reach, keep, send = pl.pallas_call(
        functools.partial(local_kernel, count),
        grid=(2,),
        in_specs=[
            smem(),
            full((count, rows_dev)),
            half(x_width),
            half(bc_width),
            pl.BlockSpec((1, LEAD, x_width + bc_width), lambda h: (h, 0, 0)),
            full((taps, x_width)),
            full((taps, bc_width)),
            half(heads),
            full((1, heads)),
            full((2 * heads, x_width)),
        ],
        out_specs=[half(x_width), half(x_width), half(groups * 2 * rows), half(heads), packed_spec, packed_spec],
        out_shape=[
            jax.ShapeDtypeStruct((rows_dev, x_width), BF),
            jax.ShapeDtypeStruct((rows_dev, x_width), BF),
            jax.ShapeDtypeStruct((rows_dev, groups * 2 * rows), BF),
            jax.ShapeDtypeStruct((rows_dev, heads), F32),
            jax.ShapeDtypeStruct((2, pack_rows, x_group), BF),
            jax.ShapeDtypeStruct((2, pack_rows, x_group), BF),
        ],
        scratch_shapes=[pltpu.VMEM((rows + LEAD, x_group), F32)],
        cost_estimate=pl.CostEstimate(flops=400_000_000, bytes_accessed=6 << 20, transcendentals=700_000),
        name="local_states",
    )(
        ids, docs, ssm_input, bc, lead, conv_input, conv_bc.reshape(taps, -1), step_size,
        decay_rate.reshape(1, heads), expand,
    )

    other = swap(send, 1)
    chip = pl.pallas_call(
        join_kernel,
        in_specs=[smem(), vmem(), vmem()],
        out_specs=vmem(),
        out_shape=jax.ShapeDtypeStruct(keep.shape, BF),
        name="join_states",
    )(ids, keep, other)
    chip_pieces = two_way_gather(chip[:1], chip[1:], chip)
    chips = count // 2
    state_shape = jax.ShapeDtypeStruct((2, STATE, x_group), BF)
    enter_mine, enter_other = pl.pallas_call(
        functools.partial(enter_kernel, [(p, part) for p, part, _ in chip_pieces], count),
        in_specs=[smem(), vmem(), vmem()] + [anywhere()] * len(chip_pieces),
        out_specs=[vmem(), vmem()],
        out_shape=[state_shape, state_shape],
        scratch_shapes=[
            pltpu.VMEM((chips, pack_rows, x_group), BF),
            pltpu.VMEM((chips, pack_rows, x_group), BF),
            pltpu.SemaphoreType.DMA((2 * chips,)),
            pltpu.VMEM((STATE, x_group), F32),
        ],
        name="enter_states",
    )(ids, keep, other, *[array for _, _, array in chip_pieces])
    enter_got = swap(enter_other, 1)

    pair = [(i, i ^ 1) for i in range(4)]
    front_send, front_keep = attend(ids, docs, queries, out_weight, pieces, False)
    front_sum = front_keep + lax.ppermute(front_send, "head", pair)
    front_got = lax.ppermute(front_sum, "head", [(2, 0), (3, 1)])
    back_send, back_keep = attend(ids, docs, queries, out_weight, pieces, True)
    back_sum = back_keep + lax.ppermute(back_send, "head", pair)
    back_got = lax.ppermute(back_sum, "head", [(0, 2), (1, 3)])
    attn_out = jnp.where(z < 2, front_sum + front_got, back_sum + back_got)

    state_spec = pl.BlockSpec((1, STATE, x_group), lambda h: (h, 0, 0))
    skip = jnp.broadcast_to(skip_gain.reshape(1, heads), (8, heads))
    ssm_out = pl.pallas_call(
        finish_kernel,
        grid=(2,),
        in_specs=[
            smem(),
            half(x_width),
            half(x_width),
            half(groups * 2 * rows),
            half(heads),
            full((8, heads)),
            full((2 * heads, x_width)),
            state_spec,
            state_spec,
        ],
        out_specs=half(x_width),
        out_shape=jax.ShapeDtypeStruct((rows_dev, x_width), BF),
        scratch_shapes=[pltpu.VMEM((2 * rows, x_group), BF)],
        cost_estimate=pl.CostEstimate(flops=300_000_000, bytes_accessed=5 << 20, transcendentals=0),
        name="finish",
    )(ids, xc, xt, mix, reach, skip, expand, enter_mine, enter_got)
    return (attn_out, ssm_out)


def solution(mesh):
    in_specs = (
        P("seq", "head"),
        P("seq", "head"),
        P("seq", "head"),
        P("head", None),
        P("seq", "head"),
        P("seq", None, "head"),
        P(None, "head"),
        P(None, None, "head"),
        P("seq", "head"),
        P("head"),
        P("head"),
        P("seq"),
    )
    out_specs = (P(("seq", "head"), None), P("seq", "head"))
    return jax.shard_map(shards, mesh=mesh, in_specs=in_specs, out_specs=out_specs, check_vma=False)
```

```python
import functools
import math

import jax
import jax.numpy as jnp
import numpy as np
from jax import lax
from jax.experimental import pallas as pl
from jax.experimental.pallas import tpu as pltpu
from jax.sharding import PartitionSpec as P

HEAD_DIM = 128
STATE = 128
SB = 128
LEAD = 8
EDGE = 16
CHUNK = 512

NEG_BIG = -1e30
BF = jnp.bfloat16
F32 = jnp.float32
HI = lax.Precision.HIGHEST


def anywhere():
    return pl.BlockSpec(memory_space=pl.ANY)


def vmem():
    return pl.BlockSpec(memory_space=pltpu.VMEM)


def params(mebibytes):
    return pltpu.CompilerParams(vmem_limit_bytes=mebibytes << 20)


def takes(microseconds):
    return pl.CostEstimate(
        flops=int(microseconds * 1e10), bytes_accessed=int(microseconds * 3.7e6), transcendentals=0
    )


def in_hbm(x):
    return pltpu.with_memory_space_constraint(x, pltpu.HBM)


def swap(x, bit):
    count = lax.axis_size("seq")
    return lax.ppermute(x, "seq", [(i, i ^ bit) for i in range(count)])


def chip_gather(whole):
    count = lax.axis_size("seq")
    return [(0, whole)] + [(pattern, swap(whole, pattern)) for pattern in range(2, count, 2)]


def assemble(places, count, pieces, kvs, docs_ref, lead_ref):
    me = lax.axis_index("seq")
    rows = kvs.shape[0] // (2 * count)
    for piece, pattern in zip(pieces, places):
        owner = lax.bitwise_xor(me, pattern)
        back = 2 * count - 1 - owner
        kvs[pl.ds(pl.multiple_of(owner * rows, rows), rows), :] = piece[:rows]
        kvs[pl.ds(pl.multiple_of(back * rows, rows), rows), :] = piece[rows + EDGE : 2 * rows + EDGE]
        front_edge = piece[rows : rows + EDGE]
        docs_ref[pl.ds(owner, 1), :] = front_edge[:, : 2 * rows].astype(F32)[EDGE - 1 :]

        @pl.when(owner == me - 1)
        def _(front_edge=front_edge):
            lead_ref[0] = front_edge

        @pl.when(owner == me + 1)
        def _(piece=piece):
            lead_ref[1] = piece[2 * rows + EDGE :]

    own_edge = pieces[0][rows : rows + EDGE]

    @pl.when(me == 0)
    def _():
        lead_ref[0] = own_edge

    @pl.when(me == count - 1)
    def _():
        lead_ref[1] = own_edge


def attend_kernel(places, count, part, q_ref, w_ref, *rest):
    if part == 0:
        total = len(places)
        send_ref, keep_ref, kvs, docs_all, lead_ref, scores, top, acc, ctx = rest[total:]
        assemble(places, count, rest[:total], kvs, docs_all, lead_ref)
    else:
        kvs, docs_all, _, send_ref, keep_ref, scores, top, acc, ctx = rest
    me = lax.axis_index("seq")
    odd = lax.rem(lax.axis_index("head"), 2)
    rows = q_ref.shape[0] // 2
    chunk = rows // 2
    own_rows = chunk // 2
    kv_heads = kvs.shape[1] // (2 * HEAD_DIM)
    group = q_ref.shape[1] // (kv_heads * HEAD_DIM)
    tile_rows = 2 * rows
    scale = math.log2(math.e) / math.sqrt(HEAD_DIM)
    lane = lax.broadcasted_iota(jnp.int32, docs_all.shape, 1)
    is_end = lax.rem(lane, rows) == rows - 1
    k_place = lax.broadcasted_iota(jnp.int32, (chunk, tile_rows), 1)
    q_local = lax.broadcasted_iota(jnp.int32, (chunk, tile_rows), 0)
    q_local = q_local + part * own_rows + jnp.where(q_local >= own_rows, own_rows, 0)
    for side in range(2):
        block = 2 * count - 1 - me if side else me
        own = docs_all[pl.ds(lax.shift_right_logical(block, 1), 1), :]
        own = jnp.where(lax.rem(block, 2) == 1, own[:, rows:], own[:, :rows])
        own_col = jnp.transpose(jnp.broadcast_to(own, (rows, rows)))[:, :1]
        picks = [slice(c * chunk + part * own_rows, c * chunk + (part + 1) * own_rows) for c in range(2)]
        own_col = jnp.concatenate([own_col[pick] for pick in picks], axis=0)
        over = is_end & (docs_all[...] < own[:, :1])
        start = jnp.sum(over.astype(F32)).astype(jnp.int32)
        first_tile = lax.shift_right_logical(start, 1)
        last_tile = lax.shift_right_logical(block, 1) + 1
        q_place = block * rows + q_local
        heads = [list(range(kv * group, (kv + 1) * group)) for kv in range(kv_heads)]
        qs = [
            jnp.concatenate(
                [
                    q_ref[side * rows + pick.start : side * rows + pick.stop, h * HEAD_DIM : (h + 1) * HEAD_DIM]
                    for h in heads[kv]
                    for pick in picks
                ],
                axis=0,
            )
            for kv in range(kv_heads)
        ]
        top[...] = jnp.full(top.shape, NEG_BIG, F32)
        acc[...] = jnp.zeros(acc.shape, F32)

        def score_step(tile, carry, qs=qs, q_place=q_place, own_col=own_col):
            at = pl.multiple_of(tile * tile_rows, tile_rows)
            docs = docs_all[pl.ds(tile, 1), :]
            allowed = (k_place + at <= q_place) & (docs == own_col)
            for kv in range(kv_heads):
                keys = kvs[pl.ds(at, tile_rows), kv * HEAD_DIM : (kv + 1) * HEAD_DIM]
                found = lax.dot_general(
                    qs[kv], keys, (((1,), (1,)), ((), ())), preferred_element_type=F32
                )
                found = jnp.where(
                    allowed[None], found.reshape(group, chunk, tile_rows), NEG_BIG
                ).reshape(group * chunk, tile_rows)
                scores[tile, kv] = found
                top[kv] = jnp.maximum(
                    top[kv], jnp.maximum(found[:, :HEAD_DIM], found[:, HEAD_DIM:])
                )
            return carry

        lax.fori_loop(first_tile, last_tile, score_step, 0)
        row_tops = [jnp.max(top[kv], axis=1, keepdims=True) for kv in range(kv_heads)]

        def mix_step(tile, carry, row_tops=row_tops):
            at = pl.multiple_of(tile * tile_rows, tile_rows)
            for kv in range(kv_heads):
                first = (kv_heads + kv) * HEAD_DIM
                values = kvs[pl.ds(at, tile_rows), first : first + HEAD_DIM]
                values = jnp.concatenate([values, jnp.ones_like(values)], axis=1)
                weights = jnp.exp2((scores[tile, kv] - row_tops[kv]) * scale).astype(BF)
                acc[kv] += jnp.dot(weights, values, preferred_element_type=F32)
            return carry

        lax.fori_loop(first_tile, last_tile, mix_step, 0)
        for kv in range(kv_heads):
            mixed = (acc[kv, :, :HEAD_DIM] / acc[kv, :, HEAD_DIM:]).astype(BF)
            for e, h in enumerate(heads[kv]):
                ctx[side * chunk : (side + 1) * chunk, h * HEAD_DIM : (h + 1) * HEAD_DIM] = mixed[
                    e * chunk : (e + 1) * chunk
                ]
    mixed = ctx[...]
    columns = w_ref.shape[1]
    made = [
        jnp.dot(mixed, w_ref[:, at : at + 256], preferred_element_type=F32).astype(BF)
        for at in range(0, columns, 256)
    ]

    def put(low_ref, high_ref):
        for at, got in enumerate(made):
            lanes = slice(at * 256, (at + 1) * 256)
            for side in range(2):
                first = 2 * side * own_rows
                low_ref[side * own_rows : (side + 1) * own_rows, lanes] = got[first : first + own_rows]
                high_ref[side * own_rows : (side + 1) * own_rows, lanes] = got[
                    first + own_rows : first + 2 * own_rows
                ]

    @pl.when(odd == 0)
    def _():
        put(keep_ref, send_ref)

    @pl.when(odd == 1)
    def _():
        put(send_ref, keep_ref)


def attend(queries, out_weight, part, places, operands):
    count = lax.axis_size("seq")
    rows = queries.shape[0] // 2
    chunk = rows // 2
    kv_width = operands[0].shape[1]
    kv_heads = kv_width // (2 * HEAD_DIM)
    group = queries.shape[1] // (kv_heads * HEAD_DIM)
    columns = out_weight.shape[1]
    outs = [jax.ShapeDtypeStruct((chunk, columns), BF)] * 2
    if part == 0:
        specs = [vmem()] * len(operands)
        outs = outs + [
            pltpu.VMEM((2 * count * rows, kv_width), BF),
            pltpu.VMEM((count, 2 * rows), F32),
            pltpu.VMEM((2, EDGE, kv_width), BF),
        ]
    else:
        specs = [vmem(), vmem(), anywhere()]
    return pl.pallas_call(
        functools.partial(attend_kernel, places, count, part),
        in_specs=[vmem()] * 2 + specs,
        out_specs=[vmem()] * len(outs),
        out_shape=outs,
        scratch_shapes=[
            pltpu.VMEM((count, kv_heads, group * chunk, 2 * rows), F32),
            pltpu.VMEM((kv_heads, group * chunk, HEAD_DIM), F32),
            pltpu.VMEM((kv_heads, group * chunk, 2 * HEAD_DIM), F32),
            pltpu.VMEM((rows, queries.shape[1]), BF),
        ],
        compiler_params=params(8 + count * 7 // 8),
        cost_estimate=takes(8),
        name="attend_late" if part else "attend_early",
    )(queries, out_weight, *operands)


def pair_kernel(got_ref, keep_ref, after_ref, send_out, keep_out, *through):
    for ref in through:
        ref[...] = after_ref[...]
    own_rows = send_out.shape[0]
    low = lax.axis_index("head") < 2

    def add(first):
        rows = slice(first, first + own_rows)
        return (got_ref[rows].astype(F32) + keep_ref[rows].astype(F32)).astype(BF)

    @pl.when(low)
    def _():
        keep_out[...] = add(0)
        send_out[...] = add(own_rows)

    @pl.when(jnp.logical_not(low))
    def _():
        keep_out[...] = add(own_rows)
        send_out[...] = add(0)


def pair_sum(got, keep, after, through):
    rows, columns = keep.shape
    outs = [jax.ShapeDtypeStruct((rows // 2, columns), BF)] * 2
    if through:
        outs = outs + [jax.ShapeDtypeStruct(after.shape, after.dtype)]
    return pl.pallas_call(
        pair_kernel,
        in_specs=[vmem(), vmem(), vmem() if through else anywhere()],
        out_specs=[vmem()] * len(outs),
        out_shape=outs,
        compiler_params=params(8),
        cost_estimate=takes(0),
        name="pair_sum",
    )(got, keep, after)


def last_kernel(early_got, early_keep, late_got, late_keep, after_ref, out_ref):
    rows = early_got.shape[0]
    out_ref[:rows] = (early_got[...].astype(F32) + early_keep[...].astype(F32)).astype(BF)
    out_ref[rows:] = (late_got[...].astype(F32) + late_keep[...].astype(F32)).astype(BF)


def prepare_kernel(k_ref, v_ref, docs_ref, xf_ref, xb_ref, bc_ref, kv_ref, flat_ref):
    rows = k_ref.shape[0] // 2
    width = k_ref.shape[1]
    part = bc_ref.shape[2]
    for at in range(2):
        flat_ref[:, at * part : (at + 1) * part] = bc_ref[:, at, :]
    docs = jnp.broadcast_to(docs_ref[...], (LEAD, 2 * rows)).astype(F32)[:1]
    docs = jnp.concatenate([docs, jnp.zeros((1, 2 * width - 2 * rows), F32)], axis=1)
    for half, x_ref in ((0, xf_ref), (1, xb_ref)):
        first = half * (rows + EDGE)
        kv_ref[first : first + rows, :width] = k_ref[half * rows : (half + 1) * rows]
        kv_ref[first : first + rows, width:] = v_ref[half * rows : (half + 1) * rows]
        x_edge = x_ref[...].astype(F32)
        bc_edge = flat_ref[(half + 1) * rows - LEAD : (half + 1) * rows].astype(F32)
        lines = []
        for t in range(LEAD - 3, LEAD):
            for edge in (x_edge, bc_edge):
                lines += [edge[t : t + 1, c : c + CHUNK] for c in range(0, edge.shape[1], CHUNK)]
        kv_ref[first + rows : first + rows + EDGE] = jnp.concatenate(lines + [docs], axis=0).astype(BF)


def load_kernel(w_ref, q_ref, x_ref, kv_ref, w_out, q_out, x_out, kv_out, sems):
    copies = [
        pltpu.make_async_copy(q_ref, q_out, sems.at[0]),
        pltpu.make_async_copy(x_ref, x_out, sems.at[5]),
    ]
    parts = 4
    size = w_ref.shape[0] // parts
    for at in range(parts):
        piece = pl.ds(at * size, size)
        copies.append(pltpu.make_async_copy(w_ref.at[piece], w_out.at[piece], sems.at[at + 1]))
    for copy in copies:
        copy.start()
    kv_out[...] = kv_ref[...]
    for copy in copies:
        copy.wait()


def spread(values, expand):
    high = values.astype(BF)
    low = (values - high.astype(F32)).astype(BF)
    return jnp.dot(jnp.concatenate([high, low], axis=1), expand, preferred_element_type=F32)


def local_kernel(
    count, docs_ref, lead_ref, x_ref, bc_ref, tx_ref, tbc_ref, step_ref, rate_ref, expand_ref, after_ref,
    xc_ref, xt_ref, mix_ref, reach_ref, keep_ref, send_ref, ext,
):
    half = pl.program_id(0)
    me = lax.axis_index("seq")
    core = lax.rem(me, 2)
    rows = xc_ref.shape[0]
    x_width = x_ref.shape[1]
    mine = pl.ds(pl.multiple_of(half * rows, rows), rows)
    bc_width = bc_ref.shape[1]
    groups = bc_width // (2 * STATE)
    x_group = x_width // groups
    block = jnp.where(half == 0, me, 2 * count - 1 - me)

    def doc_row(where):
        got = docs_ref[pl.ds(lax.shift_right_logical(where, 1), 1), :]
        return jnp.where(lax.rem(where, 2) == 1, got[:, rows:], got[:, :rows])

    own = doc_row(block)
    before = jnp.where(block > 0, doc_row(jnp.maximum(block - 1, 0)), -1.0)
    lead = lead_ref[half].astype(F32)
    chunks = (x_width + bc_width) // CHUNK
    lane = lax.broadcasted_iota(jnp.int32, (1, rows), 1)
    own_b = jnp.broadcast_to(own, (8, rows))
    before_b = jnp.broadcast_to(before, (8, rows))
    lane_b = jnp.broadcast_to(lane, (8, rows))
    lines = []
    for k in range(1, 4):
        moved = jnp.where(lane_b < k, pltpu.roll(before_b, k, 1), pltpu.roll(own_b, k, 1))
        lines.append((moved == own_b)[:1].astype(F32))
    last_doc = before[:, rows - 1 :]
    end_doc = own[:, rows - 1 :]
    lines.append((own == end_doc).astype(F32))
    lines.append((own == last_doc).astype(F32))
    lines.append(own)
    lines.append(jnp.zeros((2, rows), F32))
    table = jnp.transpose(jnp.concatenate(lines, axis=0))
    same = [table[:, k : k + 1] for k in range(3)]
    ending, alive, own_col = table[:, 3:4], table[:, 4:5], table[:, 5:6]

    def conv(source, taps, chunk, width):
        for t in range(3):
            for c in range(width // CHUNK):
                line = t * chunks + chunk + c
                ext[LEAD - 3 + t : LEAD - 2 + t, c * CHUNK : (c + 1) * CHUNK] = lead[line : line + 1]
        ext[LEAD:, :width] = source.astype(F32)
        total = ext[LEAD:, :width] * taps[0:1]
        for k in range(1, 4):
            total += same[k - 1] * (ext[LEAD - k : LEAD - k + rows, :width] * taps[k : k + 1])
        return (total * (0.5 * jnp.tanh(0.5 * total) + 0.5)).astype(BF)

    tbc = jnp.concatenate([tbc_ref[:, 0, :], tbc_ref[:, 1, :]], axis=1)
    bc = conv(bc_ref[mine, :], tbc, x_width // CHUNK, bc_width)
    row_id = lax.broadcasted_iota(jnp.int32, (rows, rows), 0)
    col_id = lax.broadcasted_iota(jnp.int32, (rows, rows), 1)
    lower = row_id >= col_id
    steps = jnp.transpose(step_ref[...])
    logs = jnp.dot(
        lower.astype(F32), -rate_ref[...] * steps, preferred_element_type=F32, precision=HI
    )
    grow = jnp.exp(-logs) * steps
    reach = jnp.exp(logs)
    reach_ref[...] = reach
    expand = expand_ref[...]
    fade_end = spread(reach[rows - 8 :], expand)[7:8]
    carries = jnp.max(jnp.where(end_doc == last_doc, 1.0, 0.0))
    fade = fade_end * carries
    fade_high = fade.astype(BF)
    fade_low = (fade - fade_high.astype(F32)).astype(BF)
    allowed = lower & (own_col == own)
    for g in range(groups):
        lanes = slice(g * x_group, (g + 1) * x_group)
        xc = conv(x_ref[mine, lanes], tx_ref[:, lanes], g * x_group // CHUNK, x_group)
        xc_ref[:, lanes] = xc
        xt = (xc.astype(F32) * spread(grow, expand[:, lanes])).astype(BF)
        xt_ref[:, lanes] = xt
        b = bc[:, g * STATE : (g + 1) * STATE]
        c = bc[:, (groups + g) * STATE : (groups + g + 1) * STATE]
        cb = lax.dot_general(c, b, (((1,), (1,)), ((), ())), preferred_element_type=F32)
        mix_ref[:, g * 2 * rows : g * 2 * rows + rows] = jnp.where(allowed, cb, 0.0).astype(BF)
        mix_ref[:, g * 2 * rows + rows : (g + 1) * 2 * rows] = (c.astype(F32) * alive).astype(BF)
        b_t = jnp.transpose(b.astype(F32) * ending).astype(BF)
        state = jnp.dot(b_t, xt, preferred_element_type=F32) * fade_end[:, lanes]
        packed = jnp.concatenate(
            [
                state.astype(BF),
                jnp.broadcast_to(fade_high[:, lanes], (8, x_group)),
                jnp.broadcast_to(fade_low[:, lanes], (8, x_group)),
            ],
            axis=0,
        )

        @pl.when(core == g)
        def _(packed=packed):
            keep_ref[0] = packed

        @pl.when(core != g)
        def _(packed=packed):
            send_ref[0] = packed


def unpack(packed):
    state = packed[:STATE].astype(F32)
    fade = packed[STATE : STATE + 1].astype(F32) + packed[STATE + 8 : STATE + 9].astype(F32)
    return fade, state


def pack(fade, state):
    high = fade.astype(BF)
    low = (fade - high.astype(F32)).astype(BF)
    shape = (8, state.shape[1])
    return jnp.concatenate(
        [state.astype(BF), jnp.broadcast_to(high, shape), jnp.broadcast_to(low, shape)], axis=0
    )


def join_kernel(mine_ref, other_ref, after_ref, out_ref):
    core = lax.rem(lax.axis_index("seq"), 2)
    for half in range(2):
        first_is_mine = core == half

        def joined(first, second):
            fade_a, state_a = unpack(first)
            fade_b, state_b = unpack(second)
            return pack(fade_a * fade_b, fade_b * state_a + state_b)

        @pl.when(first_is_mine)
        def _(half=half):
            out_ref[half] = joined(mine_ref[half], other_ref[half])

        @pl.when(jnp.logical_not(first_is_mine))
        def _(half=half):
            out_ref[half] = joined(other_ref[half], mine_ref[half])


def enter_kernel(places, count, mine_ref, other_ref, after_ref, *rest):
    total = len(places)
    pieces = rest[:total]
    keep_ref, send_ref, fronts, backs, sems, run = rest[total:]
    me = lax.axis_index("seq")
    core = lax.rem(me, 2)
    chip = lax.shift_right_logical(me, 1)
    chips = count // 2
    copies = []
    for at, pattern in enumerate(places):
        slot = lax.bitwise_xor(chip, pattern // 2)
        for half, target in enumerate((fronts, backs)):
            copy = pltpu.make_async_copy(pieces[at].at[half], target.at[slot], sems.at[len(copies)])
            copy.start()
            copies.append(copy)
    for copy in copies:
        copy.wait()
    run[...] = jnp.zeros(run.shape, F32)

    def put(half):
        entering = run[...]
        mine_first = core == half

        def after(packed):
            fade, state = unpack(packed)
            return (fade * entering + state).astype(BF)

        @pl.when(mine_first)
        def _():
            keep_ref[half] = entering.astype(BF)
            send_ref[half] = after(mine_ref[half])

        @pl.when(jnp.logical_not(mine_first))
        def _():
            send_ref[half] = entering.astype(BF)
            keep_ref[half] = after(other_ref[half])

    def front_step(at, carry):
        @pl.when(at == chip)
        def _():
            put(0)

        fade, state = unpack(fronts[at])
        run[...] = fade * run[...] + state
        return carry

    lax.fori_loop(0, chips, front_step, 0)

    def back_step(k, carry):
        at = chips - 1 - k

        @pl.when(at == chip)
        def _():
            put(1)

        fade, state = unpack(backs[at])
        run[...] = fade * run[...] + state
        return carry

    lax.fori_loop(0, chips - chip, back_step, 0)


def finish_kernel(
    xc_ref, xt_ref, mix_ref, reach_ref, skip_ref, expand_ref, mine_ref, other_ref, out_ref, done_ref, both
):
    done_ref[...] = jnp.zeros(done_ref.shape, F32)
    core = lax.rem(lax.axis_index("seq"), 2)
    half = pl.program_id(0)
    rows, x_width = out_ref.shape
    groups = mix_ref.shape[1] // (2 * rows)
    x_group = x_width // groups
    for g in range(groups):
        lanes = slice(g * x_group, (g + 1) * x_group)
        expand = expand_ref[:, lanes]
        both[:rows] = xt_ref[:, lanes]

        @pl.when(core == g)
        def _():
            both[rows:] = mine_ref[half]

        @pl.when(core != g)
        def _():
            both[rows:] = other_ref[half]

        mix = mix_ref[:, g * 2 * rows : (g + 1) * 2 * rows]
        made = jnp.dot(mix, both[...], preferred_element_type=F32)
        made = made * spread(reach_ref[...], expand)
        skip = spread(jnp.broadcast_to(skip_ref[...], (8, skip_ref.shape[1])), expand)[:1]
        out_ref[:, lanes] = (made + skip * xc_ref[:, lanes].astype(F32)).astype(BF)


def shards(
    queries, key_rows, value_rows, out_weight, ssm_input, bc_input, conv_input, conv_bc, step_size,
    decay_rate, skip_gain, doc_ids,
):
    count = lax.axis_size("seq")
    rows_dev = queries.shape[0]
    rows = rows_dev // 2
    x_width = ssm_input.shape[1]
    bc_width = bc_input.shape[1] * bc_input.shape[2]
    taps = conv_input.shape[0]
    groups = bc_width // (2 * STATE)
    heads = decay_rate.shape[0]
    x_group = x_width // groups

    docs = doc_ids.reshape(1, rows_dev)
    row_block = rows // LEAD
    kv, bc = pl.pallas_call(
        prepare_kernel,
        grid=(1,),
        in_specs=[
            vmem(),
            vmem(),
            vmem(),
            pl.BlockSpec((LEAD, x_width), lambda t: (row_block - 1, 0)),
            pl.BlockSpec((LEAD, x_width), lambda t: (2 * row_block - 1, 0)),
            vmem(),
        ],
        out_specs=[vmem()] * 2,
        out_shape=[
            jax.ShapeDtypeStruct((rows_dev + 2 * EDGE, 2 * key_rows.shape[1]), BF),
            pltpu.VMEM((rows_dev, bc_width), BF),
        ],
        compiler_params=params(12),
        name="prepare",
    )(in_hbm(key_rows), in_hbm(value_rows), docs, in_hbm(ssm_input), in_hbm(ssm_input), in_hbm(bc_input))

    weight, query_rows, x_rows, kv_again = pl.pallas_call(
        load_kernel,
        in_specs=[anywhere()] * 3 + [vmem()],
        out_specs=[vmem()] * 4,
        out_shape=[
            pltpu.VMEM(out_weight.shape, BF),
            pltpu.VMEM(queries.shape, BF),
            pltpu.VMEM(ssm_input.shape, BF),
            jax.ShapeDtypeStruct(kv.shape, BF),
        ],
        scratch_shapes=[pltpu.SemaphoreType.DMA((6,))],
        compiler_params=params(10),
        cost_estimate=takes(5),
        name="load",
    )(in_hbm(out_weight), in_hbm(queries), in_hbm(ssm_input), kv)

    pieces = chip_gather(kv)
    pieces = pieces + [(1, swap(kv_again, 1))] + [(pattern ^ 1, swap(array, 1)) for pattern, array in pieces[1:]]

    expand = np.repeat(np.eye(heads, dtype=np.float32), x_width // heads, axis=1)
    expand = jnp.asarray(np.concatenate([expand, expand], axis=0), BF)
    pack_rows = STATE + 16
    full = lambda shape: pl.BlockSpec(shape, lambda h: (0,) * len(shape))
    half = lambda width: pl.BlockSpec((rows, width), lambda h: (h, 0))
    packed_spec = pl.BlockSpec((1, pack_rows, x_group), lambda h: (h, 0, 0))
    pair = [(i, i ^ 1) for i in range(4)]
    cross = [(i, i ^ 2) for i in range(4)]
    early_send, early_keep, kvs, docs_all, lead = attend(
        query_rows, weight, 0, [pattern for pattern, _ in pieces], [array for _, array in pieces]
    )
    early_pair = lax.ppermute(early_send, "head", pair)
    late_send, late_keep = attend(query_rows, weight, 1, None, [kvs, docs_all, early_keep])
    late_pair = lax.ppermute(late_send, "head", pair)
    xc, xt, mix, reach, keep, send = pl.pallas_call(
        functools.partial(local_kernel, count),
        grid=(2,),
        in_specs=[
            vmem(),
            vmem(),
            vmem(),
            vmem(),
            full((taps, x_width)),
            full(conv_bc.shape),
            pl.BlockSpec((heads, rows), lambda h: (0, h)),
            full((1, heads)),
            full((2 * heads, x_width)),
            anywhere(),
        ],
        out_specs=[half(x_width), half(x_width), half(groups * 2 * rows), half(heads), packed_spec, packed_spec],
        out_shape=[
            pltpu.HBM((rows_dev, x_width), BF),
            pltpu.HBM((rows_dev, x_width), BF),
            pltpu.HBM((rows_dev, groups * 2 * rows), BF),
            pltpu.HBM((rows_dev, heads), F32),
            jax.ShapeDtypeStruct((2, pack_rows, x_group), BF),
            jax.ShapeDtypeStruct((2, pack_rows, x_group), BF),
        ],
        scratch_shapes=[pltpu.VMEM((rows + LEAD, x_group), F32)],
        cost_estimate=takes(5.5),
        compiler_params=params(16 + count // 4),
        name="local_states",
    )(
        docs_all, lead, x_rows, bc, in_hbm(conv_input), in_hbm(conv_bc), in_hbm(step_size.T),
        decay_rate.reshape(1, heads), expand, late_keep,
    )

    early_cross, early_mine, send = pair_sum(early_pair, early_keep, send, True)
    other = swap(send, 1)
    early_got = lax.ppermute(early_cross, "head", cross)
    chip = pl.pallas_call(
        join_kernel,
        in_specs=[vmem(), vmem(), anywhere()],
        out_specs=vmem(),
        out_shape=jax.ShapeDtypeStruct(keep.shape, BF),
        compiler_params=params(12),
        cost_estimate=takes(0),
        name="join_states",
    )(keep, other, late_keep)
    late_cross, late_mine = pair_sum(late_pair, late_keep, early_got, False)
    late_got = lax.ppermute(late_cross, "head", cross)
    chip_pieces = chip_gather(chip)
    chips = count // 2
    state_shape = jax.ShapeDtypeStruct((2, STATE, x_group), BF)
    enter_mine, enter_other = pl.pallas_call(
        functools.partial(enter_kernel, [pattern for pattern, _ in chip_pieces], count),
        in_specs=[vmem(), vmem()] + [anywhere()] * (1 + len(chip_pieces)),
        out_specs=[vmem(), vmem()],
        out_shape=[state_shape, state_shape],
        scratch_shapes=[
            pltpu.VMEM((chips, pack_rows, x_group), BF),
            pltpu.VMEM((chips, pack_rows, x_group), BF),
            pltpu.SemaphoreType.DMA((2 * chips,)),
            pltpu.VMEM((STATE, x_group), F32),
        ],
        compiler_params=params(14 + chips),
        cost_estimate=takes(0),
        name="enter_states",
    )(keep, other, late_got, *[array for _, array in chip_pieces])
    enter_got = swap(enter_other, 1)

    ssm_out, finished = pl.pallas_call(
        finish_kernel,
        grid=(2,),
        in_specs=[
            half(x_width),
            half(x_width),
            half(groups * 2 * rows),
            half(heads),
            full((1, heads)),
            full((2 * heads, x_width)),
            vmem(),
            vmem(),
        ],
        out_specs=[half(x_width), full((8, 128))],
        out_shape=[pltpu.HBM((rows_dev, x_width), BF), jax.ShapeDtypeStruct((8, 128), F32)],
        scratch_shapes=[pltpu.VMEM((2 * rows, x_group), BF)],
        cost_estimate=takes(0),
        compiler_params=params(20),
        name="finish",
    )(xc, xt, mix, reach, skip_gain.reshape(1, heads), expand, enter_mine, enter_got)
    attn_out = pl.pallas_call(
        last_kernel,
        in_specs=[vmem()] * 4 + [anywhere()],
        out_specs=vmem(),
        out_shape=jax.ShapeDtypeStruct((rows // 2, out_weight.shape[1]), BF),
        compiler_params=params(6),
        cost_estimate=takes(0),
        name="last_sum",
    )(early_got, early_mine, late_got, late_mine, finished)
    return (attn_out, ssm_out)


def solution(mesh):
    in_specs = (
        P("seq", "head"),
        P("seq", "head"),
        P("seq", "head"),
        P("head", None),
        P("seq", "head"),
        P("seq", None, "head"),
        P(None, "head"),
        P(None, None, "head"),
        P("seq", "head"),
        P("head"),
        P("head"),
        P("seq"),
    )
    out_specs = (P(("seq", "head"), None), P("seq", "head"))
    return jax.shard_map(shards, mesh=mesh, in_specs=in_specs, out_specs=out_specs, check_vma=False)
```

```python
import functools
import math

import jax
import jax.numpy as jnp
import numpy as np
from jax import lax
from jax.experimental import pallas as pl
from jax.experimental.pallas import tpu as pltpu
from jax.sharding import PartitionSpec as P

HEAD_DIM = 128
STATE = 128
SB = 128
LEAD = 8
EDGE = 16
CHUNK = 512

NEG_BIG = -1e30
BF = jnp.bfloat16
F32 = jnp.float32
HI = lax.Precision.HIGHEST


def anywhere():
    return pl.BlockSpec(memory_space=pl.ANY)


def vmem():
    return pl.BlockSpec(memory_space=pltpu.VMEM)


def params(mebibytes):
    return pltpu.CompilerParams(vmem_limit_bytes=mebibytes << 20)


def takes(microseconds):
    return pl.CostEstimate(
        flops=int(microseconds * 1e10), bytes_accessed=int(microseconds * 3.7e6), transcendentals=0
    )


def in_hbm(x):
    return pltpu.with_memory_space_constraint(x, pltpu.HBM)


def swap(x, bit):
    count = lax.axis_size("seq")
    return lax.ppermute(x, "seq", [(i, i ^ bit) for i in range(count)])


def chip_gather(whole):
    count = lax.axis_size("seq")
    return [(0, whole)] + [(pattern, swap(whole, pattern)) for pattern in range(2, count, 2)]


def assemble(places, count, pieces, kvs, docs_ref, lead_ref):
    me = lax.axis_index("seq")
    rows = kvs.shape[0] // (2 * count)
    for piece, pattern in zip(pieces, places):
        owner = lax.bitwise_xor(me, pattern)
        back = 2 * count - 1 - owner
        kvs[pl.ds(pl.multiple_of(owner * rows, rows), rows), :] = piece[:rows]
        kvs[pl.ds(pl.multiple_of(back * rows, rows), rows), :] = piece[rows + EDGE : 2 * rows + EDGE]
        front_edge = piece[rows : rows + EDGE]
        docs_ref[pl.ds(owner, 1), :] = front_edge[:, : 2 * rows].astype(F32)[EDGE - 1 :]

        @pl.when(owner == me - 1)
        def _(front_edge=front_edge):
            lead_ref[0] = front_edge

        @pl.when(owner == me + 1)
        def _(piece=piece):
            lead_ref[1] = piece[2 * rows + EDGE :]

    own_edge = pieces[0][rows : rows + EDGE]

    @pl.when(me == 0)
    def _():
        lead_ref[0] = own_edge

    @pl.when(me == count - 1)
    def _():
        lead_ref[1] = own_edge


def attend_kernel(places, count, part, q_ref, w_ref, *rest):
    if part == 0:
        total = len(places)
        send_ref, keep_ref, kvs, docs_all, lead_ref, scores, top, acc, ctx = rest[total:]
        assemble(places, count, rest[:total], kvs, docs_all, lead_ref)
    else:
        kvs, docs_all, _, send_ref, keep_ref, scores, top, acc, ctx = rest
    me = lax.axis_index("seq")
    odd = lax.rem(lax.axis_index("head"), 2)
    rows = q_ref.shape[0] // 2
    chunk = rows // 2
    own_rows = chunk // 2
    kv_heads = kvs.shape[1] // (2 * HEAD_DIM)
    group = q_ref.shape[1] // (kv_heads * HEAD_DIM)
    tile_rows = 2 * rows
    scale = math.log2(math.e) / math.sqrt(HEAD_DIM)
    lane = lax.broadcasted_iota(jnp.int32, docs_all.shape, 1)
    is_end = lax.rem(lane, rows) == rows - 1
    k_place = lax.broadcasted_iota(jnp.int32, (chunk, tile_rows), 1)
    q_local = lax.broadcasted_iota(jnp.int32, (chunk, tile_rows), 0)
    q_local = q_local + part * own_rows + jnp.where(q_local >= own_rows, own_rows, 0)
    for side in range(2):
        block = 2 * count - 1 - me if side else me
        own = docs_all[pl.ds(lax.shift_right_logical(block, 1), 1), :]
        own = jnp.where(lax.rem(block, 2) == 1, own[:, rows:], own[:, :rows])
        own_col = jnp.transpose(jnp.broadcast_to(own, (rows, rows)))[:, :1]
        picks = [slice(c * chunk + part * own_rows, c * chunk + (part + 1) * own_rows) for c in range(2)]
        own_col = jnp.concatenate([own_col[pick] for pick in picks], axis=0)
        over = is_end & (docs_all[...] < own[:, :1])
        start = jnp.sum(over.astype(F32)).astype(jnp.int32)
        first_tile = lax.shift_right_logical(start, 1)
        last_tile = lax.shift_right_logical(block, 1) + 1
        q_place = block * rows + q_local
        heads = [list(range(kv * group, (kv + 1) * group)) for kv in range(kv_heads)]
        qs = [
            jnp.concatenate(
                [
                    q_ref[side * rows + pick.start : side * rows + pick.stop, h * HEAD_DIM : (h + 1) * HEAD_DIM]
                    for h in heads[kv]
                    for pick in picks
                ],
                axis=0,
            )
            for kv in range(kv_heads)
        ]
        top[...] = jnp.full(top.shape, NEG_BIG, F32)
        acc[...] = jnp.zeros(acc.shape, F32)

        def score_step(tile, carry, qs=qs, q_place=q_place, own_col=own_col):
            at = pl.multiple_of(tile * tile_rows, tile_rows)
            docs = docs_all[pl.ds(tile, 1), :]
            allowed = (k_place + at <= q_place) & (docs == own_col)
            for kv in range(kv_heads):
                keys = kvs[pl.ds(at, tile_rows), kv * HEAD_DIM : (kv + 1) * HEAD_DIM]
                found = lax.dot_general(
                    qs[kv], keys, (((1,), (1,)), ((), ())), preferred_element_type=F32
                )
                found = jnp.where(
                    allowed[None], found.reshape(group, chunk, tile_rows), NEG_BIG
                ).reshape(group * chunk, tile_rows)
                scores[tile, kv] = found
                top[kv] = jnp.maximum(
                    top[kv], jnp.maximum(found[:, :HEAD_DIM], found[:, HEAD_DIM:])
                )
            return carry

        lax.fori_loop(first_tile, last_tile, score_step, 0)
        row_tops = [jnp.max(top[kv], axis=1, keepdims=True) for kv in range(kv_heads)]

        def mix_step(tile, carry, row_tops=row_tops):
            at = pl.multiple_of(tile * tile_rows, tile_rows)
            for kv in range(kv_heads):
                first = (kv_heads + kv) * HEAD_DIM
                values = kvs[pl.ds(at, tile_rows), first : first + HEAD_DIM]
                values = jnp.concatenate([values, jnp.ones_like(values)], axis=1)
                weights = jnp.exp2((scores[tile, kv] - row_tops[kv]) * scale).astype(BF)
                acc[kv] += jnp.dot(weights, values, preferred_element_type=F32)
            return carry

        lax.fori_loop(first_tile, last_tile, mix_step, 0)
        for kv in range(kv_heads):
            mixed = (acc[kv, :, :HEAD_DIM] / acc[kv, :, HEAD_DIM:]).astype(BF)
            for e, h in enumerate(heads[kv]):
                ctx[side * chunk : (side + 1) * chunk, h * HEAD_DIM : (h + 1) * HEAD_DIM] = mixed[
                    e * chunk : (e + 1) * chunk
                ]
    mixed = ctx[...]
    columns = w_ref.shape[1]
    made = [
        jnp.dot(mixed, w_ref[:, at : at + 256], preferred_element_type=F32).astype(BF)
        for at in range(0, columns, 256)
    ]

    def put(low_ref, high_ref):
        for at, got in enumerate(made):
            lanes = slice(at * 256, (at + 1) * 256)
            for side in range(2):
                first = 2 * side * own_rows
                low_ref[side * own_rows : (side + 1) * own_rows, lanes] = got[first : first + own_rows]
                high_ref[side * own_rows : (side + 1) * own_rows, lanes] = got[
                    first + own_rows : first + 2 * own_rows
                ]

    @pl.when(odd == 0)
    def _():
        put(keep_ref, send_ref)

    @pl.when(odd == 1)
    def _():
        put(send_ref, keep_ref)


def attend(queries, out_weight, part, places, operands):
    count = lax.axis_size("seq")
    rows = queries.shape[0] // 2
    chunk = rows // 2
    kv_width = operands[0].shape[1]
    kv_heads = kv_width // (2 * HEAD_DIM)
    group = queries.shape[1] // (kv_heads * HEAD_DIM)
    columns = out_weight.shape[1]
    outs = [jax.ShapeDtypeStruct((chunk, columns), BF)] * 2
    if part == 0:
        specs = [vmem()] * len(operands)
        outs = outs + [
            pltpu.VMEM((2 * count * rows, kv_width), BF),
            pltpu.VMEM((count, 2 * rows), F32),
            pltpu.VMEM((2, EDGE, kv_width), BF),
        ]
    else:
        specs = [vmem(), vmem(), anywhere()]
    return pl.pallas_call(
        functools.partial(attend_kernel, places, count, part),
        in_specs=[vmem()] * 2 + specs,
        out_specs=[vmem()] * len(outs),
        out_shape=outs,
        scratch_shapes=[
            pltpu.VMEM((count, kv_heads, group * chunk, 2 * rows), F32),
            pltpu.VMEM((kv_heads, group * chunk, HEAD_DIM), F32),
            pltpu.VMEM((kv_heads, group * chunk, 2 * HEAD_DIM), F32),
            pltpu.VMEM((rows, queries.shape[1]), BF),
        ],
        compiler_params=params(8 + count * 7 // 8),
        cost_estimate=takes(8),
        name="attend_late" if part else "attend_early",
    )(queries, out_weight, *operands)


def pair_kernel(got_ref, keep_ref, after_ref, send_out, keep_out, *through):
    for ref in through:
        ref[...] = after_ref[...]
    own_rows = send_out.shape[0]
    low = lax.axis_index("head") < 2

    def add(first):
        rows = slice(first, first + own_rows)
        return (got_ref[rows].astype(F32) + keep_ref[rows].astype(F32)).astype(BF)

    @pl.when(low)
    def _():
        keep_out[...] = add(0)
        send_out[...] = add(own_rows)

    @pl.when(jnp.logical_not(low))
    def _():
        keep_out[...] = add(own_rows)
        send_out[...] = add(0)


def pair_sum(got, keep, after, through):
    rows, columns = keep.shape
    outs = [jax.ShapeDtypeStruct((rows // 2, columns), BF)] * 2
    if through:
        outs = outs + [jax.ShapeDtypeStruct(after.shape, after.dtype)]
    return pl.pallas_call(
        pair_kernel,
        in_specs=[vmem(), vmem(), vmem() if through else anywhere()],
        out_specs=[vmem()] * len(outs),
        out_shape=outs,
        compiler_params=params(8),
        cost_estimate=takes(0),
        name="pair_sum",
    )(got, keep, after)


def last_kernel(early_got, early_keep, late_got, late_keep, after_ref, out_ref, done_ref):
    done_ref[...] = jnp.zeros(done_ref.shape, F32)
    rows = early_got.shape[0]
    out_ref[:rows] = (early_got[...].astype(F32) + early_keep[...].astype(F32)).astype(BF)
    out_ref[rows:] = (late_got[...].astype(F32) + late_keep[...].astype(F32)).astype(BF)


def prepare_kernel(k_ref, v_ref, docs_ref, xf_ref, xb_ref, bf_ref, bb_ref, kv_ref):
    rows = k_ref.shape[0] // 2
    width = k_ref.shape[1]
    docs = jnp.broadcast_to(docs_ref[...], (LEAD, 2 * rows)).astype(F32)[:1]
    docs = jnp.concatenate([docs, jnp.zeros((1, 2 * width - 2 * rows), F32)], axis=1)
    for half, x_ref, bc_ref in ((0, xf_ref, bf_ref), (1, xb_ref, bb_ref)):
        first = half * (rows + EDGE)
        kv_ref[first : first + rows, :width] = k_ref[half * rows : (half + 1) * rows]
        kv_ref[first : first + rows, width:] = v_ref[half * rows : (half + 1) * rows]
        x_edge = x_ref[...].astype(F32)
        bc_edge = jnp.concatenate([bc_ref[:, 0, :], bc_ref[:, 1, :]], axis=1).astype(F32)
        lines = []
        for t in range(LEAD - 3, LEAD):
            for edge in (x_edge, bc_edge):
                lines += [edge[t : t + 1, c : c + CHUNK] for c in range(0, edge.shape[1], CHUNK)]
        kv_ref[first + rows : first + rows + EDGE] = jnp.concatenate(lines + [docs], axis=0).astype(BF)


def load_kernel(w_ref, q_ref, x_ref, bc_ref, kv_ref, w_out, q_out, x_out, bc_out, kv_out, bc_in, sems):
    bc_copy = pltpu.make_async_copy(bc_ref, bc_in, sems.at[6])
    bc_copy.start()
    copies = [
        pltpu.make_async_copy(q_ref, q_out, sems.at[0]),
        pltpu.make_async_copy(x_ref, x_out, sems.at[5]),
    ]
    parts = 4
    size = w_ref.shape[0] // parts
    for at in range(parts):
        piece = pl.ds(at * size, size)
        copies.append(pltpu.make_async_copy(w_ref.at[piece], w_out.at[piece], sems.at[at + 1]))
    for copy in copies:
        copy.start()
    kv_out[...] = kv_ref[...]
    bc_copy.wait()
    part = bc_in.shape[2]
    for at in range(2):
        bc_out[:, at * part : (at + 1) * part] = bc_in[:, at, :]
    for copy in copies:
        copy.wait()


def spread(values, expand):
    high = values.astype(BF)
    low = (values - high.astype(F32)).astype(BF)
    return jnp.dot(jnp.concatenate([high, low], axis=1), expand, preferred_element_type=F32)


def local_kernel(
    count, docs_ref, lead_ref, x_ref, bc_ref, tx_ref, tbc_ref, step_ref, rate_ref, expand_ref, after_ref,
    xc_ref, xt_ref, mix_ref, reach_ref, keep_ref, send_ref, ext,
):
    half = pl.program_id(0)
    me = lax.axis_index("seq")
    core = lax.rem(me, 2)
    rows = xc_ref.shape[0]
    x_width = x_ref.shape[1]
    mine = pl.ds(pl.multiple_of(half * rows, rows), rows)
    bc_width = bc_ref.shape[1]
    groups = bc_width // (2 * STATE)
    x_group = x_width // groups
    block = jnp.where(half == 0, me, 2 * count - 1 - me)

    def doc_row(where):
        got = docs_ref[pl.ds(lax.shift_right_logical(where, 1), 1), :]
        return jnp.where(lax.rem(where, 2) == 1, got[:, rows:], got[:, :rows])

    own = doc_row(block)
    before = jnp.where(block > 0, doc_row(jnp.maximum(block - 1, 0)), -1.0)
    lead = lead_ref[half].astype(F32)
    chunks = (x_width + bc_width) // CHUNK
    lane = lax.broadcasted_iota(jnp.int32, (1, rows), 1)
    own_b = jnp.broadcast_to(own, (8, rows))
    before_b = jnp.broadcast_to(before, (8, rows))
    lane_b = jnp.broadcast_to(lane, (8, rows))
    lines = []
    for k in range(1, 4):
        moved = jnp.where(lane_b < k, pltpu.roll(before_b, k, 1), pltpu.roll(own_b, k, 1))
        lines.append((moved == own_b)[:1].astype(F32))
    last_doc = before[:, rows - 1 :]
    end_doc = own[:, rows - 1 :]
    lines.append((own == end_doc).astype(F32))
    lines.append((own == last_doc).astype(F32))
    lines.append(own)
    lines.append(jnp.zeros((2, rows), F32))
    table = jnp.transpose(jnp.concatenate(lines, axis=0))
    same = [table[:, k : k + 1] for k in range(3)]
    ending, alive, own_col = table[:, 3:4], table[:, 4:5], table[:, 5:6]

    def conv(source, taps, chunk, width):
        for t in range(3):
            for c in range(width // CHUNK):
                line = t * chunks + chunk + c
                ext[LEAD - 3 + t : LEAD - 2 + t, c * CHUNK : (c + 1) * CHUNK] = lead[line : line + 1]
        ext[LEAD:, :width] = source.astype(F32)
        total = ext[LEAD:, :width] * taps[0:1]
        for k in range(1, 4):
            total += same[k - 1] * (ext[LEAD - k : LEAD - k + rows, :width] * taps[k : k + 1])
        return (total * (0.5 * jnp.tanh(0.5 * total) + 0.5)).astype(BF)

    tbc = jnp.concatenate([tbc_ref[:, 0, :], tbc_ref[:, 1, :]], axis=1)
    bc = conv(bc_ref[mine, :], tbc, x_width // CHUNK, bc_width)
    row_id = lax.broadcasted_iota(jnp.int32, (rows, rows), 0)
    col_id = lax.broadcasted_iota(jnp.int32, (rows, rows), 1)
    lower = row_id >= col_id
    steps = jnp.transpose(step_ref[...])
    logs = jnp.dot(
        lower.astype(F32), -rate_ref[...] * steps, preferred_element_type=F32, precision=HI
    )
    grow = jnp.exp(-logs) * steps
    reach = jnp.exp(logs)
    reach_ref[...] = reach
    expand = expand_ref[...]
    fade_end = spread(reach[rows - 8 :], expand)[7:8]
    carries = jnp.max(jnp.where(end_doc == last_doc, 1.0, 0.0))
    fade = fade_end * carries
    allowed = lower & (own_col == own)
    for g in range(groups):
        lanes = slice(g * x_group, (g + 1) * x_group)
        xc = conv(x_ref[mine, lanes], tx_ref[:, lanes], g * x_group // CHUNK, x_group)
        xc_ref[:, lanes] = xc
        xt = (xc.astype(F32) * spread(grow, expand[:, lanes])).astype(BF)
        xt_ref[:, lanes] = xt
        b = bc[:, g * STATE : (g + 1) * STATE]
        c = bc[:, (groups + g) * STATE : (groups + g + 1) * STATE]
        cb = lax.dot_general(c, b, (((1,), (1,)), ((), ())), preferred_element_type=F32)
        mix_ref[:, g * 2 * rows : g * 2 * rows + rows] = jnp.where(allowed, cb, 0.0).astype(BF)
        mix_ref[:, g * 2 * rows + rows : (g + 1) * 2 * rows] = (c.astype(F32) * alive).astype(BF)
        b_t = jnp.transpose(b.astype(F32) * ending).astype(BF)
        state = jnp.dot(b_t, xt, preferred_element_type=F32) * fade_end[:, lanes]
        state = state.astype(BF)
        tail = fade_rows(fade[:, lanes])

        @pl.when(core == g)
        def _(state=state, tail=tail):
            keep_ref[0, :STATE] = state
            keep_ref[0, STATE:] = tail

        @pl.when(core != g)
        def _(state=state, tail=tail):
            send_ref[0, :STATE] = state
            send_ref[0, STATE:] = tail


def unpack(packed):
    state = packed[:STATE].astype(F32)
    tail = packed[STATE : STATE + LEAD].astype(F32)
    return tail[:1] + tail[LEAD - 1 :], state


def fade_rows(fade):
    high = fade.astype(BF).astype(F32)
    shape = (LEAD // 2, fade.shape[1])
    parts = [jnp.broadcast_to(high, shape), jnp.broadcast_to(fade - high, shape)]
    return jnp.concatenate(parts, axis=0).astype(BF)


def join_kernel(mine_ref, other_ref, after_ref, out_ref):
    core = lax.rem(lax.axis_index("seq"), 2)
    for half in range(2):
        first_is_mine = core == half

        def joined(first, second, half=half):
            fade_a, state_a = unpack(first)
            fade_b, state_b = unpack(second)
            out_ref[half, :STATE] = (fade_b * state_a + state_b).astype(BF)
            out_ref[half, STATE:] = fade_rows(fade_a * fade_b)

        @pl.when(first_is_mine)
        def _(half=half):
            joined(mine_ref[half], other_ref[half])

        @pl.when(jnp.logical_not(first_is_mine))
        def _(half=half):
            joined(other_ref[half], mine_ref[half])


def enter_kernel(places, count, mine_ref, other_ref, after_ref, *rest):
    total = len(places)
    pieces = rest[:total]
    keep_ref, send_ref, fronts, backs, sems, run = rest[total:]
    me = lax.axis_index("seq")
    core = lax.rem(me, 2)
    chip = lax.shift_right_logical(me, 1)
    chips = count // 2
    copies = []
    for at, pattern in enumerate(places):
        slot = lax.bitwise_xor(chip, pattern // 2)
        for half, target in enumerate((fronts, backs)):
            copy = pltpu.make_async_copy(pieces[at].at[half], target.at[slot], sems.at[len(copies)])
            copy.start()
            copies.append(copy)
    for copy in copies:
        copy.wait()
    run[...] = jnp.zeros(run.shape, F32)

    def put(half):
        entering = run[...]
        mine_first = core == half

        def after(packed):
            fade, state = unpack(packed)
            return (fade * entering + state).astype(BF)

        @pl.when(mine_first)
        def _():
            keep_ref[half] = entering.astype(BF)
            send_ref[half] = after(mine_ref[half])

        @pl.when(jnp.logical_not(mine_first))
        def _():
            send_ref[half] = entering.astype(BF)
            keep_ref[half] = after(other_ref[half])

    def front_step(at, carry):
        @pl.when(at == chip)
        def _():
            put(0)

        fade, state = unpack(fronts[at])
        run[...] = fade * run[...] + state
        return carry

    lax.fori_loop(0, chips, front_step, 0)

    def back_step(k, carry):
        at = chips - 1 - k

        @pl.when(at == chip)
        def _():
            put(1)

        fade, state = unpack(backs[at])
        run[...] = fade * run[...] + state
        return carry

    lax.fori_loop(0, chips - chip, back_step, 0)


def finish_kernel(
    xc_ref, xt_ref, mix_ref, reach_ref, skip_ref, expand_ref, mine_ref, other_ref, after_ref, out_ref, both
):
    core = lax.rem(lax.axis_index("seq"), 2)
    half = pl.program_id(0)
    rows, x_width = out_ref.shape
    groups = mix_ref.shape[1] // (2 * rows)
    x_group = x_width // groups
    for g in range(groups):
        lanes = slice(g * x_group, (g + 1) * x_group)
        expand = expand_ref[:, lanes]
        both[:rows] = xt_ref[:, lanes]

        @pl.when(core == g)
        def _():
            both[rows:] = mine_ref[half]

        @pl.when(core != g)
        def _():
            both[rows:] = other_ref[half]

        mix = mix_ref[:, g * 2 * rows : (g + 1) * 2 * rows]
        made = jnp.dot(mix, both[...], preferred_element_type=F32)
        made = made * spread(reach_ref[...], expand)
        skip = spread(jnp.broadcast_to(skip_ref[...], (8, skip_ref.shape[1])), expand)[:1]
        out_ref[:, lanes] = (made + skip * xc_ref[:, lanes].astype(F32)).astype(BF)


def shards(
    queries, key_rows, value_rows, out_weight, ssm_input, bc_input, conv_input, conv_bc, step_size,
    decay_rate, skip_gain, doc_ids,
):
    count = lax.axis_size("seq")
    rows_dev = queries.shape[0]
    rows = rows_dev // 2
    x_width = ssm_input.shape[1]
    bc_width = bc_input.shape[1] * bc_input.shape[2]
    taps = conv_input.shape[0]
    groups = bc_width // (2 * STATE)
    heads = decay_rate.shape[0]
    x_group = x_width // groups

    docs = doc_ids.reshape(1, rows_dev)
    row_block = rows // LEAD
    kv = pl.pallas_call(
        prepare_kernel,
        grid=(1,),
        in_specs=[
            vmem(),
            vmem(),
            vmem(),
            pl.BlockSpec((LEAD, x_width), lambda t: (row_block - 1, 0)),
            pl.BlockSpec((LEAD, x_width), lambda t: (2 * row_block - 1, 0)),
            pl.BlockSpec((LEAD,) + bc_input.shape[1:], lambda t: (row_block - 1, 0, 0)),
            pl.BlockSpec((LEAD,) + bc_input.shape[1:], lambda t: (2 * row_block - 1, 0, 0)),
        ],
        out_specs=vmem(),
        out_shape=jax.ShapeDtypeStruct((rows_dev + 2 * EDGE, 2 * key_rows.shape[1]), BF),
        compiler_params=params(12),
        name="prepare",
    )(
        in_hbm(key_rows), in_hbm(value_rows), in_hbm(docs), in_hbm(ssm_input), in_hbm(ssm_input),
        in_hbm(bc_input), in_hbm(bc_input),
    )

    weight, query_rows, x_rows, bc, kv_again = pl.pallas_call(
        load_kernel,
        in_specs=[anywhere()] * 4 + [vmem()],
        out_specs=[vmem()] * 5,
        out_shape=[
            pltpu.VMEM(out_weight.shape, BF),
            pltpu.VMEM(queries.shape, BF),
            pltpu.VMEM(ssm_input.shape, BF),
            pltpu.VMEM((rows_dev, bc_width), BF),
            jax.ShapeDtypeStruct(kv.shape, BF),
        ],
        scratch_shapes=[pltpu.VMEM(bc_input.shape, BF), pltpu.SemaphoreType.DMA((7,))],
        compiler_params=params(10),
        cost_estimate=takes(5),
        name="load",
    )(in_hbm(out_weight), in_hbm(queries), in_hbm(ssm_input), in_hbm(bc_input), kv)

    pieces = chip_gather(kv)
    pieces = pieces + [(1, swap(kv_again, 1))] + [(pattern ^ 1, swap(array, 1)) for pattern, array in pieces[1:]]

    expand = np.repeat(np.eye(heads, dtype=np.float32), x_width // heads, axis=1)
    expand = jnp.asarray(np.concatenate([expand, expand], axis=0), BF)
    pack_rows = STATE + LEAD
    full = lambda shape: pl.BlockSpec(shape, lambda h: (0,) * len(shape))
    half = lambda width: pl.BlockSpec((rows, width), lambda h: (h, 0))
    packed_spec = pl.BlockSpec((1, pack_rows, x_group), lambda h: (h, 0, 0))
    pair = [(i, i ^ 1) for i in range(4)]
    cross = [(i, i ^ 2) for i in range(4)]
    early_send, early_keep, kvs, docs_all, lead = attend(
        query_rows, weight, 0, [pattern for pattern, _ in pieces], [array for _, array in pieces]
    )
    early_pair = lax.ppermute(early_send, "head", pair)
    late_send, late_keep = attend(query_rows, weight, 1, None, [kvs, docs_all, early_keep])
    late_pair = lax.ppermute(late_send, "head", pair)
    xc, xt, mix, reach, keep, send = pl.pallas_call(
        functools.partial(local_kernel, count),
        grid=(2,),
        in_specs=[
            vmem(),
            vmem(),
            vmem(),
            vmem(),
            full((taps, x_width)),
            full(conv_bc.shape),
            pl.BlockSpec((heads, rows), lambda h: (0, h)),
            full((1, heads)),
            full((2 * heads, x_width)),
            anywhere(),
        ],
        out_specs=[half(x_width), half(x_width), half(groups * 2 * rows), half(heads), packed_spec, packed_spec],
        out_shape=[
            pltpu.HBM((rows_dev, x_width), BF),
            pltpu.HBM((rows_dev, x_width), BF),
            pltpu.HBM((rows_dev, groups * 2 * rows), BF),
            pltpu.HBM((rows_dev, heads), F32),
            jax.ShapeDtypeStruct((2, pack_rows, x_group), BF),
            jax.ShapeDtypeStruct((2, pack_rows, x_group), BF),
        ],
        scratch_shapes=[pltpu.VMEM((rows + LEAD, x_group), F32)],
        cost_estimate=takes(5.5),
        compiler_params=params(16 + count // 4),
        name="local_states",
    )(
        docs_all, lead, x_rows, bc, in_hbm(conv_input), in_hbm(conv_bc), in_hbm(step_size.T),
        decay_rate.reshape(1, heads), expand, late_keep,
    )

    early_cross, early_mine, send = pair_sum(early_pair, early_keep, send, True)
    other = swap(send, 1)
    early_got = lax.ppermute(early_cross, "head", cross)
    chip = pl.pallas_call(
        join_kernel,
        in_specs=[vmem(), vmem(), anywhere()],
        out_specs=vmem(),
        out_shape=jax.ShapeDtypeStruct(keep.shape, BF),
        compiler_params=params(12),
        cost_estimate=takes(0),
        name="join_states",
    )(keep, other, late_keep)
    late_cross, late_mine = pair_sum(late_pair, late_keep, early_got, False)
    late_got = lax.ppermute(late_cross, "head", cross)
    chip_pieces = chip_gather(chip)
    chips = count // 2
    state_shape = jax.ShapeDtypeStruct((2, STATE, x_group), BF)
    enter_mine, enter_other = pl.pallas_call(
        functools.partial(enter_kernel, [pattern for pattern, _ in chip_pieces], count),
        in_specs=[vmem(), vmem()] + [anywhere()] * (1 + len(chip_pieces)),
        out_specs=[vmem(), vmem()],
        out_shape=[state_shape, state_shape],
        scratch_shapes=[
            pltpu.VMEM((chips, pack_rows, x_group), BF),
            pltpu.VMEM((chips, pack_rows, x_group), BF),
            pltpu.SemaphoreType.DMA((2 * chips,)),
            pltpu.VMEM((STATE, x_group), F32),
        ],
        compiler_params=params(14 + chips),
        cost_estimate=takes(0),
        name="enter_states",
    )(keep, other, late_got, *[array for _, array in chip_pieces])
    enter_got = swap(enter_other, 1)

    attn_out, summed = pl.pallas_call(
        last_kernel,
        in_specs=[vmem()] * 4 + [anywhere()],
        out_specs=[vmem()] * 2,
        out_shape=[
            jax.ShapeDtypeStruct((rows // 2, out_weight.shape[1]), BF),
            jax.ShapeDtypeStruct((8, 128), F32),
        ],
        compiler_params=params(6),
        cost_estimate=takes(0),
        name="last_sum",
    )(early_got, early_mine, late_got, late_mine, enter_other)
    ssm_out = pl.pallas_call(
        finish_kernel,
        grid=(2,),
        in_specs=[
            half(x_width),
            half(x_width),
            half(groups * 2 * rows),
            half(heads),
            full((1, heads)),
            full((2 * heads, x_width)),
            vmem(),
            vmem(),
            anywhere(),
        ],
        out_specs=half(x_width),
        out_shape=pltpu.HBM((rows_dev, x_width), BF),
        scratch_shapes=[pltpu.VMEM((2 * rows, x_group), BF)],
        cost_estimate=takes(0),
        compiler_params=params(20),
        name="finish",
    )(xc, xt, mix, reach, skip_gain.reshape(1, heads), expand, enter_mine, enter_got, summed)
    return (attn_out, ssm_out)


def solution(mesh):
    in_specs = (
        P("seq", "head"),
        P("seq", "head"),
        P("seq", "head"),
        P("head", None),
        P("seq", "head"),
        P("seq", None, "head"),
        P(None, "head"),
        P(None, None, "head"),
        P("seq", "head"),
        P("head"),
        P("head"),
        P("seq"),
    )
    out_specs = (P(("seq", "head"), None), P("seq", "head"))
    return jax.shard_map(shards, mesh=mesh, in_specs=in_specs, out_specs=out_specs, check_vma=False)
```

```python
import functools
import math

import jax
import jax.numpy as jnp
import numpy as np
from jax import lax
from jax.experimental import pallas as pl
from jax.experimental.pallas import tpu as pltpu
from jax.sharding import PartitionSpec as P

HEAD_DIM = 128
STATE = 128
SB = 128
LEAD = 8
EDGE = 16
CHUNK = 512

NEG_BIG = -1e30
BF = jnp.bfloat16
F32 = jnp.float32
HI = lax.Precision.HIGHEST


def anywhere():
    return pl.BlockSpec(memory_space=pl.ANY)


def vmem():
    return pl.BlockSpec(memory_space=pltpu.VMEM)


def params(mebibytes):
    return pltpu.CompilerParams(vmem_limit_bytes=mebibytes << 20)


def takes(microseconds):
    return pl.CostEstimate(
        flops=int(microseconds * 1e10), bytes_accessed=int(microseconds * 3.7e6), transcendentals=0
    )


def in_hbm(x):
    return pltpu.with_memory_space_constraint(x, pltpu.HBM)


def swap(x, bit):
    count = lax.axis_size("seq")
    return lax.ppermute(x, "seq", [(i, i ^ bit) for i in range(count)])


def chip_gather(whole):
    count = lax.axis_size("seq")
    return [(0, whole)] + [(pattern, swap(whole, pattern)) for pattern in range(2, count, 2)]


def assemble(places, count, pieces, kvs, docs_ref, lead_ref):
    me = lax.axis_index("seq")
    rows = kvs.shape[0] // (2 * count)
    for piece, pattern in zip(pieces, places):
        owner = lax.bitwise_xor(me, pattern)
        back = 2 * count - 1 - owner
        kvs[pl.ds(pl.multiple_of(owner * rows, rows), rows), :] = piece[:rows]
        kvs[pl.ds(pl.multiple_of(back * rows, rows), rows), :] = piece[rows + EDGE : 2 * rows + EDGE]
        front_edge = piece[rows : rows + EDGE]
        docs_ref[pl.ds(owner, 1), :] = front_edge[:, : 2 * rows].astype(F32)[EDGE - 1 :]

        @pl.when(owner == me - 1)
        def _(front_edge=front_edge):
            lead_ref[0] = front_edge

        @pl.when(owner == me + 1)
        def _(piece=piece):
            lead_ref[1] = piece[2 * rows + EDGE :]

    own_edge = pieces[0][rows : rows + EDGE]

    @pl.when(me == 0)
    def _():
        lead_ref[0] = own_edge

    @pl.when(me == count - 1)
    def _():
        lead_ref[1] = own_edge


def attend_kernel(places, count, part, q_ref, w_ref, *rest):
    if part == 0:
        total = len(places)
        send_ref, keep_ref, kvs, docs_all, lead_ref, scores, top, acc, ctx = rest[total:]
        assemble(places, count, rest[:total], kvs, docs_all, lead_ref)
    else:
        kvs, docs_all, _, send_ref, keep_ref, scores, top, acc, ctx = rest
    me = lax.axis_index("seq")
    odd = lax.rem(lax.axis_index("head"), 2)
    rows = q_ref.shape[0] // 2
    chunk = rows // 2
    own_rows = chunk // 2
    kv_heads = kvs.shape[1] // (2 * HEAD_DIM)
    group = q_ref.shape[1] // (kv_heads * HEAD_DIM)
    tile_rows = 2 * rows
    scale = math.log2(math.e) / math.sqrt(HEAD_DIM)
    lane = lax.broadcasted_iota(jnp.int32, docs_all.shape, 1)
    is_end = lax.rem(lane, rows) == rows - 1
    k_place = lax.broadcasted_iota(jnp.int32, (chunk, tile_rows), 1)
    q_local = lax.broadcasted_iota(jnp.int32, (chunk, tile_rows), 0)
    q_local = q_local + part * own_rows + jnp.where(q_local >= own_rows, own_rows, 0)
    for side in range(2):
        block = 2 * count - 1 - me if side else me
        own = docs_all[pl.ds(lax.shift_right_logical(block, 1), 1), :]
        own = jnp.where(lax.rem(block, 2) == 1, own[:, rows:], own[:, :rows])
        own_col = jnp.transpose(jnp.broadcast_to(own, (rows, rows)))[:, :1]
        picks = [slice(c * chunk + part * own_rows, c * chunk + (part + 1) * own_rows) for c in range(2)]
        own_col = jnp.concatenate([own_col[pick] for pick in picks], axis=0)
        over = is_end & (docs_all[...] < own[:, :1])
        start = jnp.sum(over.astype(F32)).astype(jnp.int32)
        first_tile = lax.shift_right_logical(start, 1)
        last_tile = lax.shift_right_logical(block, 1) + 1
        q_place = block * rows + q_local
        heads = [list(range(kv * group, (kv + 1) * group)) for kv in range(kv_heads)]
        qs = [
            jnp.concatenate(
                [
                    q_ref[side * rows + pick.start : side * rows + pick.stop, h * HEAD_DIM : (h + 1) * HEAD_DIM]
                    for h in heads[kv]
                    for pick in picks
                ],
                axis=0,
            )
            for kv in range(kv_heads)
        ]
        top[...] = jnp.full(top.shape, NEG_BIG, F32)
        acc[...] = jnp.zeros(acc.shape, F32)

        def score_step(tile, carry, qs=qs, q_place=q_place, own_col=own_col):
            at = pl.multiple_of(tile * tile_rows, tile_rows)
            docs = docs_all[pl.ds(tile, 1), :]
            allowed = (k_place + at <= q_place) & (docs == own_col)
            for kv in range(kv_heads):
                keys = kvs[pl.ds(at, tile_rows), kv * HEAD_DIM : (kv + 1) * HEAD_DIM]
                found = lax.dot_general(
                    qs[kv], keys, (((1,), (1,)), ((), ())), preferred_element_type=F32
                )
                found = jnp.where(
                    allowed[None], found.reshape(group, chunk, tile_rows), NEG_BIG
                ).reshape(group * chunk, tile_rows)
                scores[tile, kv] = found
                top[kv] = jnp.maximum(
                    top[kv], jnp.maximum(found[:, :HEAD_DIM], found[:, HEAD_DIM:])
                )
            return carry

        lax.fori_loop(first_tile, last_tile, score_step, 0)
        row_tops = [jnp.max(top[kv], axis=1, keepdims=True) for kv in range(kv_heads)]

        def mix_step(tile, carry, row_tops=row_tops):
            at = pl.multiple_of(tile * tile_rows, tile_rows)
            for kv in range(kv_heads):
                first = (kv_heads + kv) * HEAD_DIM
                values = kvs[pl.ds(at, tile_rows), first : first + HEAD_DIM]
                values = jnp.concatenate([values, jnp.ones_like(values)], axis=1)
                weights = jnp.exp2((scores[tile, kv] - row_tops[kv]) * scale).astype(BF)
                acc[kv] += jnp.dot(weights, values, preferred_element_type=F32)
            return carry

        lax.fori_loop(first_tile, last_tile, mix_step, 0)
        for kv in range(kv_heads):
            mixed = (acc[kv, :, :HEAD_DIM] / acc[kv, :, HEAD_DIM:]).astype(BF)
            for e, h in enumerate(heads[kv]):
                ctx[side * chunk : (side + 1) * chunk, h * HEAD_DIM : (h + 1) * HEAD_DIM] = mixed[
                    e * chunk : (e + 1) * chunk
                ]
    mixed = ctx[...]
    columns = w_ref.shape[1]
    made = [
        jnp.dot(mixed, w_ref[:, at : at + 256], preferred_element_type=F32).astype(BF)
        for at in range(0, columns, 256)
    ]

    def put(low_ref, high_ref):
        for at, got in enumerate(made):
            lanes = slice(at * 256, (at + 1) * 256)
            for side in range(2):
                first = 2 * side * own_rows
                low_ref[side * own_rows : (side + 1) * own_rows, lanes] = got[first : first + own_rows]
                high_ref[side * own_rows : (side + 1) * own_rows, lanes] = got[
                    first + own_rows : first + 2 * own_rows
                ]

    @pl.when(odd == 0)
    def _():
        put(keep_ref, send_ref)

    @pl.when(odd == 1)
    def _():
        put(send_ref, keep_ref)


def attend(queries, out_weight, part, places, operands):
    count = lax.axis_size("seq")
    rows = queries.shape[0] // 2
    chunk = rows // 2
    kv_width = operands[0].shape[1]
    kv_heads = kv_width // (2 * HEAD_DIM)
    group = queries.shape[1] // (kv_heads * HEAD_DIM)
    columns = out_weight.shape[1]
    outs = [jax.ShapeDtypeStruct((chunk, columns), BF)] * 2
    if part == 0:
        specs = [vmem()] * len(operands)
        outs = outs + [
            pltpu.VMEM((2 * count * rows, kv_width), BF),
            pltpu.VMEM((count, 2 * rows), F32),
            pltpu.VMEM((2, EDGE, kv_width), BF),
        ]
    else:
        specs = [vmem(), vmem(), anywhere()]
    return pl.pallas_call(
        functools.partial(attend_kernel, places, count, part),
        in_specs=[vmem()] * 2 + specs,
        out_specs=[vmem()] * len(outs),
        out_shape=outs,
        scratch_shapes=[
            pltpu.VMEM((count, kv_heads, group * chunk, 2 * rows), F32),
            pltpu.VMEM((kv_heads, group * chunk, HEAD_DIM), F32),
            pltpu.VMEM((kv_heads, group * chunk, 2 * HEAD_DIM), F32),
            pltpu.VMEM((rows, queries.shape[1]), BF),
        ],
        compiler_params=params(8 + count * 7 // 8),
        cost_estimate=takes(8),
        name="attend_late" if part else "attend_early",
    )(queries, out_weight, *operands)


def pair_kernel(skipped, got_ref, keep_ref, after_ref, *rest):
    send_out, keep_out, *through = rest[skipped:]
    for ref in through:
        ref[...] = after_ref[...]
    own_rows = send_out.shape[0]
    low = lax.axis_index("head") < 2

    def add(first):
        rows = slice(first, first + own_rows)
        return (got_ref[rows].astype(F32) + keep_ref[rows].astype(F32)).astype(BF)

    @pl.when(low)
    def _():
        keep_out[...] = add(0)
        send_out[...] = add(own_rows)

    @pl.when(jnp.logical_not(low))
    def _():
        keep_out[...] = add(own_rows)
        send_out[...] = add(0)


def pair_sum(got, keep, after, through, *also):
    rows, columns = keep.shape
    outs = [jax.ShapeDtypeStruct((rows // 2, columns), BF)] * 2
    if through:
        outs = outs + [jax.ShapeDtypeStruct(after.shape, after.dtype)]
    return pl.pallas_call(
        functools.partial(pair_kernel, len(also)),
        in_specs=[vmem(), vmem(), vmem() if through else anywhere()] + [anywhere()] * len(also),
        out_specs=[vmem()] * len(outs),
        out_shape=outs,
        compiler_params=params(8),
        cost_estimate=takes(0),
        name="pair_sum",
    )(got, keep, after, *also)


def last_kernel(early_got, early_keep, late_got, late_keep, after_ref, out_ref, done_ref):
    done_ref[...] = jnp.zeros(done_ref.shape, F32)
    rows = early_got.shape[0]
    out_ref[:rows] = (early_got[...].astype(F32) + early_keep[...].astype(F32)).astype(BF)
    out_ref[rows:] = (late_got[...].astype(F32) + late_keep[...].astype(F32)).astype(BF)


def prepare_kernel(k_ref, v_ref, docs_ref, xf_ref, xb_ref, bf_ref, bb_ref, kv_ref):
    rows = k_ref.shape[0] // 2
    width = k_ref.shape[1]
    docs = jnp.broadcast_to(docs_ref[...], (LEAD, 2 * rows)).astype(F32)[:1]
    docs = jnp.concatenate([docs, jnp.zeros((1, 2 * width - 2 * rows), F32)], axis=1)
    for half, x_ref, bc_ref in ((0, xf_ref, bf_ref), (1, xb_ref, bb_ref)):
        first = half * (rows + EDGE)
        kv_ref[first : first + rows, :width] = k_ref[half * rows : (half + 1) * rows]
        kv_ref[first : first + rows, width:] = v_ref[half * rows : (half + 1) * rows]
        x_edge = x_ref[...].astype(F32)
        bc_edge = jnp.concatenate([bc_ref[:, 0, :], bc_ref[:, 1, :]], axis=1).astype(F32)
        lines = []
        for t in range(LEAD - 3, LEAD):
            for edge in (x_edge, bc_edge):
                lines += [edge[t : t + 1, c : c + CHUNK] for c in range(0, edge.shape[1], CHUNK)]
        kv_ref[first + rows : first + rows + EDGE] = jnp.concatenate(lines + [docs], axis=0).astype(BF)


def load_kernel(w_ref, q_ref, x_ref, bc_ref, kv_ref, w_out, q_out, x_out, bc_out, kv_out, bc_in, sems):
    bc_copy = pltpu.make_async_copy(bc_ref, bc_in, sems.at[6])
    bc_copy.start()
    copies = [
        pltpu.make_async_copy(q_ref, q_out, sems.at[0]),
        pltpu.make_async_copy(x_ref, x_out, sems.at[5]),
    ]
    parts = 4
    size = w_ref.shape[0] // parts
    for at in range(parts):
        piece = pl.ds(at * size, size)
        copies.append(pltpu.make_async_copy(w_ref.at[piece], w_out.at[piece], sems.at[at + 1]))
    for copy in copies:
        copy.start()
    kv_out[...] = kv_ref[...]
    bc_copy.wait()
    part = bc_in.shape[2]
    for at in range(2):
        bc_out[:, at * part : (at + 1) * part] = bc_in[:, at, :]
    for copy in copies:
        copy.wait()


def spread(values, expand):
    high = values.astype(BF)
    low = (values - high.astype(F32)).astype(BF)
    return jnp.dot(jnp.concatenate([high, low], axis=1), expand, preferred_element_type=F32)


def local_kernel(
    count, docs_ref, lead_ref, x_ref, bc_ref, tx_ref, tbc_ref, step_ref, rate_ref, expand_ref, after_ref,
    xc_ref, xt_ref, mix_ref, reach_ref, keep_ref, send_ref, ext,
):
    half = pl.program_id(0)
    me = lax.axis_index("seq")
    core = lax.rem(me, 2)
    rows = xc_ref.shape[0]
    x_width = x_ref.shape[1]
    mine = pl.ds(pl.multiple_of(half * rows, rows), rows)
    bc_width = bc_ref.shape[1]
    groups = bc_width // (2 * STATE)
    x_group = x_width // groups
    block = jnp.where(half == 0, me, 2 * count - 1 - me)

    def doc_row(where):
        got = docs_ref[pl.ds(lax.shift_right_logical(where, 1), 1), :]
        return jnp.where(lax.rem(where, 2) == 1, got[:, rows:], got[:, :rows])

    own = doc_row(block)
    before = jnp.where(block > 0, doc_row(jnp.maximum(block - 1, 0)), -1.0)
    lead = lead_ref[half].astype(F32)
    chunks = (x_width + bc_width) // CHUNK
    lane = lax.broadcasted_iota(jnp.int32, (1, rows), 1)
    own_b = jnp.broadcast_to(own, (8, rows))
    before_b = jnp.broadcast_to(before, (8, rows))
    lane_b = jnp.broadcast_to(lane, (8, rows))
    lines = []
    for k in range(1, 4):
        moved = jnp.where(lane_b < k, pltpu.roll(before_b, k, 1), pltpu.roll(own_b, k, 1))
        lines.append((moved == own_b)[:1].astype(F32))
    last_doc = before[:, rows - 1 :]
    end_doc = own[:, rows - 1 :]
    lines.append((own == end_doc).astype(F32))
    lines.append((own == last_doc).astype(F32))
    lines.append(own)
    lines.append(jnp.zeros((2, rows), F32))
    table = jnp.transpose(jnp.concatenate(lines, axis=0))
    same = [table[:, k : k + 1] for k in range(3)]
    ending, alive, own_col = table[:, 3:4], table[:, 4:5], table[:, 5:6]

    def conv(source, taps, chunk, width):
        for t in range(3):
            for c in range(width // CHUNK):
                line = t * chunks + chunk + c
                ext[LEAD - 3 + t : LEAD - 2 + t, c * CHUNK : (c + 1) * CHUNK] = lead[line : line + 1]
        ext[LEAD:, :width] = source.astype(F32)
        total = ext[LEAD:, :width] * taps[0:1]
        for k in range(1, 4):
            total += same[k - 1] * (ext[LEAD - k : LEAD - k + rows, :width] * taps[k : k + 1])
        return (total * (0.5 * jnp.tanh(0.5 * total) + 0.5)).astype(BF)

    tbc = jnp.concatenate([tbc_ref[:, 0, :], tbc_ref[:, 1, :]], axis=1)
    bc = conv(bc_ref[mine, :], tbc, x_width // CHUNK, bc_width)
    row_id = lax.broadcasted_iota(jnp.int32, (rows, rows), 0)
    col_id = lax.broadcasted_iota(jnp.int32, (rows, rows), 1)
    lower = row_id >= col_id
    steps = jnp.transpose(step_ref[...])
    logs = jnp.dot(
        lower.astype(F32), -rate_ref[...] * steps, preferred_element_type=F32, precision=HI
    )
    grow = jnp.exp(-logs) * steps
    reach = jnp.exp(logs)
    reach_ref[...] = reach
    expand = expand_ref[...]
    fade_end = spread(reach[rows - 8 :], expand)[7:8]
    carries = jnp.max(jnp.where(end_doc == last_doc, 1.0, 0.0))
    fade = fade_end * carries
    allowed = lower & (own_col == own)
    for g in range(groups):
        lanes = slice(g * x_group, (g + 1) * x_group)
        xc = conv(x_ref[mine, lanes], tx_ref[:, lanes], g * x_group // CHUNK, x_group)
        xc_ref[:, lanes] = xc
        xt = (xc.astype(F32) * spread(grow, expand[:, lanes])).astype(BF)
        xt_ref[:, lanes] = xt
        b = bc[:, g * STATE : (g + 1) * STATE]
        c = bc[:, (groups + g) * STATE : (groups + g + 1) * STATE]
        cb = lax.dot_general(c, b, (((1,), (1,)), ((), ())), preferred_element_type=F32)
        mix_ref[:, g * 2 * rows : g * 2 * rows + rows] = jnp.where(allowed, cb, 0.0).astype(BF)
        mix_ref[:, g * 2 * rows + rows : (g + 1) * 2 * rows] = (c.astype(F32) * alive).astype(BF)
        b_t = jnp.transpose(b.astype(F32) * ending).astype(BF)
        state = jnp.dot(b_t, xt, preferred_element_type=F32) * fade_end[:, lanes]
        state = state.astype(BF)
        tail = fade_rows(fade[:, lanes])

        @pl.when(core == g)
        def _(state=state, tail=tail):
            keep_ref[0, :STATE] = state
            keep_ref[0, STATE:] = tail

        @pl.when(core != g)
        def _(state=state, tail=tail):
            send_ref[0, :STATE] = state
            send_ref[0, STATE:] = tail


def unpack(packed):
    state = packed[:STATE].astype(F32)
    tail = packed[STATE : STATE + LEAD].astype(F32)
    return tail[:1] + tail[LEAD - 1 :], state


def fade_rows(fade):
    high = fade.astype(BF).astype(F32)
    shape = (LEAD // 2, fade.shape[1])
    parts = [jnp.broadcast_to(high, shape), jnp.broadcast_to(fade - high, shape)]
    return jnp.concatenate(parts, axis=0).astype(BF)


def join_kernel(mine_ref, other_ref, after_ref, out_ref):
    core = lax.rem(lax.axis_index("seq"), 2)
    for half in range(2):
        first_is_mine = core == half

        def joined(first, second, half=half):
            fade_a, state_a = unpack(first)
            fade_b, state_b = unpack(second)
            out_ref[half, :STATE] = (fade_b * state_a + state_b).astype(BF)
            out_ref[half, STATE:] = fade_rows(fade_a * fade_b)

        @pl.when(first_is_mine)
        def _(half=half):
            joined(mine_ref[half], other_ref[half])

        @pl.when(jnp.logical_not(first_is_mine))
        def _(half=half):
            joined(other_ref[half], mine_ref[half])


def enter_kernel(places, count, mine_ref, other_ref, after_ref, *rest):
    total = len(places)
    pieces = rest[:total]
    keep_ref, send_ref, fronts, backs, sems, run = rest[total:]
    me = lax.axis_index("seq")
    core = lax.rem(me, 2)
    chip = lax.shift_right_logical(me, 1)
    chips = count // 2
    copies = []
    for at, pattern in enumerate(places):
        slot = lax.bitwise_xor(chip, pattern // 2)
        for half, target in enumerate((fronts, backs)):
            copy = pltpu.make_async_copy(pieces[at].at[half], target.at[slot], sems.at[len(copies)])
            copy.start()
            copies.append(copy)
    for copy in copies:
        copy.wait()
    run[...] = jnp.zeros(run.shape, F32)

    def put(half):
        entering = run[...]
        mine_first = core == half

        def after(packed):
            fade, state = unpack(packed)
            return (fade * entering + state).astype(BF)

        @pl.when(mine_first)
        def _():
            keep_ref[half] = entering.astype(BF)
            send_ref[half] = after(mine_ref[half])

        @pl.when(jnp.logical_not(mine_first))
        def _():
            send_ref[half] = entering.astype(BF)
            keep_ref[half] = after(other_ref[half])

    def front_step(at, carry):
        @pl.when(at == chip)
        def _():
            put(0)

        fade, state = unpack(fronts[at])
        run[...] = fade * run[...] + state
        return carry

    lax.fori_loop(0, chips, front_step, 0)

    def back_step(k, carry):
        at = chips - 1 - k

        @pl.when(at == chip)
        def _():
            put(1)

        fade, state = unpack(backs[at])
        run[...] = fade * run[...] + state
        return carry

    lax.fori_loop(0, chips - chip, back_step, 0)


def ready_kernel(xc_ref, xt_ref, mix_ref, reach_ref, skip_ref, expand_ref, base_ref, wide_ref):
    rows = mix_ref.shape[0] // 2
    x_width = xc_ref.shape[1]
    groups = mix_ref.shape[1] // (2 * rows)
    x_group = x_width // groups
    skip = spread(jnp.broadcast_to(skip_ref[...], (8, skip_ref.shape[1])), expand_ref[...])[:1]
    for half in range(2):
        mine = slice(half * rows, (half + 1) * rows)
        for g in range(groups):
            lanes = slice(g * x_group, (g + 1) * x_group)
            mix = mix_ref[mine, g * 2 * rows : g * 2 * rows + rows]
            made = jnp.dot(mix, xt_ref[mine, lanes], preferred_element_type=F32)
            wide = spread(reach_ref[mine, :], expand_ref[:, lanes])
            wide_ref[mine, lanes] = wide
            base_ref[mine, lanes] = made * wide + skip[:, lanes] * xc_ref[mine, lanes].astype(F32)


def finish_kernel(mix_ref, base_ref, wide_ref, mine_ref, other_ref, after_ref, out_ref):
    core = lax.rem(lax.axis_index("seq"), 2)
    half = pl.program_id(0)
    rows, x_width = out_ref.shape
    mine = pl.ds(pl.multiple_of(half * rows, rows), rows)
    groups = mix_ref.shape[1] // (2 * rows)
    x_group = x_width // groups
    for g in range(groups):
        lanes = slice(g * x_group, (g + 1) * x_group)
        reads = mix_ref[mine, g * 2 * rows + rows : (g + 1) * 2 * rows]

        def put(state, reads=reads, lanes=lanes):
            made = jnp.dot(reads, state, preferred_element_type=F32)
            out_ref[:, lanes] = (base_ref[mine, lanes] + wide_ref[mine, lanes] * made).astype(BF)

        @pl.when(core == g)
        def _(put=put):
            put(mine_ref[half])

        @pl.when(core != g)
        def _(put=put):
            put(other_ref[half])


def shards(
    queries, key_rows, value_rows, out_weight, ssm_input, bc_input, conv_input, conv_bc, step_size,
    decay_rate, skip_gain, doc_ids,
):
    count = lax.axis_size("seq")
    rows_dev = queries.shape[0]
    rows = rows_dev // 2
    x_width = ssm_input.shape[1]
    bc_width = bc_input.shape[1] * bc_input.shape[2]
    taps = conv_input.shape[0]
    groups = bc_width // (2 * STATE)
    heads = decay_rate.shape[0]
    x_group = x_width // groups

    docs = doc_ids.reshape(1, rows_dev)
    row_block = rows // LEAD
    kv = pl.pallas_call(
        prepare_kernel,
        grid=(1,),
        in_specs=[
            vmem(),
            vmem(),
            vmem(),
            pl.BlockSpec((LEAD, x_width), lambda t: (row_block - 1, 0)),
            pl.BlockSpec((LEAD, x_width), lambda t: (2 * row_block - 1, 0)),
            pl.BlockSpec((LEAD,) + bc_input.shape[1:], lambda t: (row_block - 1, 0, 0)),
            pl.BlockSpec((LEAD,) + bc_input.shape[1:], lambda t: (2 * row_block - 1, 0, 0)),
        ],
        out_specs=vmem(),
        out_shape=jax.ShapeDtypeStruct((rows_dev + 2 * EDGE, 2 * key_rows.shape[1]), BF),
        compiler_params=params(12),
        name="prepare",
    )(
        in_hbm(key_rows), in_hbm(value_rows), in_hbm(docs), in_hbm(ssm_input), in_hbm(ssm_input),
        in_hbm(bc_input), in_hbm(bc_input),
    )

    weight, query_rows, x_rows, bc, kv_again = pl.pallas_call(
        load_kernel,
        in_specs=[anywhere()] * 4 + [vmem()],
        out_specs=[vmem()] * 5,
        out_shape=[
            pltpu.VMEM(out_weight.shape, BF),
            pltpu.VMEM(queries.shape, BF),
            pltpu.VMEM(ssm_input.shape, BF),
            pltpu.VMEM((rows_dev, bc_width), BF),
            jax.ShapeDtypeStruct(kv.shape, BF),
        ],
        scratch_shapes=[pltpu.VMEM(bc_input.shape, BF), pltpu.SemaphoreType.DMA((7,))],
        compiler_params=params(10),
        cost_estimate=takes(5),
        name="load",
    )(in_hbm(out_weight), in_hbm(queries), in_hbm(ssm_input), in_hbm(bc_input), kv)

    pieces = chip_gather(kv)
    pieces = pieces + [(1, swap(kv_again, 1))] + [(pattern ^ 1, swap(array, 1)) for pattern, array in pieces[1:]]

    expand = np.repeat(np.eye(heads, dtype=np.float32), x_width // heads, axis=1)
    expand = jnp.asarray(np.concatenate([expand, expand], axis=0), BF)
    pack_rows = STATE + LEAD
    full = lambda shape: pl.BlockSpec(shape, lambda h: (0,) * len(shape))
    half = lambda width: pl.BlockSpec((rows, width), lambda h: (h, 0))
    packed_spec = pl.BlockSpec((1, pack_rows, x_group), lambda h: (h, 0, 0))
    pair = [(i, i ^ 1) for i in range(4)]
    cross = [(i, i ^ 2) for i in range(4)]
    early_send, early_keep, kvs, docs_all, lead = attend(
        query_rows, weight, 0, [pattern for pattern, _ in pieces], [array for _, array in pieces]
    )
    early_pair = lax.ppermute(early_send, "head", pair)
    late_send, late_keep = attend(query_rows, weight, 1, None, [kvs, docs_all, early_keep])
    late_pair = lax.ppermute(late_send, "head", pair)
    xc, xt, mix, reach, keep, send = pl.pallas_call(
        functools.partial(local_kernel, count),
        grid=(2,),
        in_specs=[
            vmem(),
            vmem(),
            vmem(),
            vmem(),
            full((taps, x_width)),
            full(conv_bc.shape),
            pl.BlockSpec((heads, rows), lambda h: (0, h)),
            full((1, heads)),
            full((2 * heads, x_width)),
            anywhere(),
        ],
        out_specs=[half(x_width), half(x_width), half(groups * 2 * rows), half(heads), packed_spec, packed_spec],
        out_shape=[
            pltpu.HBM((rows_dev, x_width), BF),
            pltpu.HBM((rows_dev, x_width), BF),
            pltpu.HBM((rows_dev, groups * 2 * rows), BF),
            pltpu.HBM((rows_dev, heads), F32),
            jax.ShapeDtypeStruct((2, pack_rows, x_group), BF),
            jax.ShapeDtypeStruct((2, pack_rows, x_group), BF),
        ],
        scratch_shapes=[pltpu.VMEM((rows + LEAD, x_group), F32)],
        cost_estimate=takes(5.5),
        compiler_params=params(16 + count // 4),
        name="local_states",
    )(
        docs_all, lead, x_rows, bc, in_hbm(conv_input), in_hbm(conv_bc), in_hbm(step_size.T),
        decay_rate.reshape(1, heads), expand, late_keep,
    )

    early_cross, early_mine, send = pair_sum(early_pair, early_keep, send, True)
    other = swap(send, 1)
    early_got = lax.ppermute(early_cross, "head", cross)
    chip = pl.pallas_call(
        join_kernel,
        in_specs=[vmem(), vmem(), anywhere()],
        out_specs=vmem(),
        out_shape=jax.ShapeDtypeStruct(keep.shape, BF),
        compiler_params=params(12),
        cost_estimate=takes(0),
        name="join_states",
    )(keep, other, late_keep)
    base, wide = pl.pallas_call(
        ready_kernel,
        in_specs=[vmem()] * 6,
        out_specs=[vmem()] * 2,
        out_shape=[pltpu.VMEM((rows_dev, x_width), F32)] * 2,
        cost_estimate=takes(4),
        compiler_params=params(12),
        name="ready",
    )(xc, xt, mix, reach, skip_gain.reshape(1, heads), expand)
    late_cross, late_mine = pair_sum(late_pair, late_keep, early_got, False, base)
    late_got = lax.ppermute(late_cross, "head", cross)
    chip_pieces = chip_gather(chip)
    chips = count // 2
    state_shape = jax.ShapeDtypeStruct((2, STATE, x_group), BF)
    enter_mine, enter_other = pl.pallas_call(
        functools.partial(enter_kernel, [pattern for pattern, _ in chip_pieces], count),
        in_specs=[vmem(), vmem()] + [anywhere()] * (1 + len(chip_pieces)),
        out_specs=[vmem(), vmem()],
        out_shape=[state_shape, state_shape],
        scratch_shapes=[
            pltpu.VMEM((chips, pack_rows, x_group), BF),
            pltpu.VMEM((chips, pack_rows, x_group), BF),
            pltpu.SemaphoreType.DMA((2 * chips,)),
            pltpu.VMEM((STATE, x_group), F32),
        ],
        compiler_params=params(14 + chips),
        cost_estimate=takes(0),
        name="enter_states",
    )(keep, other, late_got, *[array for _, array in chip_pieces])
    enter_got = swap(enter_other, 1)

    attn_out, summed = pl.pallas_call(
        last_kernel,
        in_specs=[vmem()] * 4 + [anywhere()],
        out_specs=[vmem()] * 2,
        out_shape=[
            jax.ShapeDtypeStruct((rows // 2, out_weight.shape[1]), BF),
            jax.ShapeDtypeStruct((8, 128), F32),
        ],
        compiler_params=params(6),
        cost_estimate=takes(0),
        name="last_sum",
    )(early_got, early_mine, late_got, late_mine, enter_other)
    ssm_out = pl.pallas_call(
        finish_kernel,
        grid=(2,),
        in_specs=[vmem()] * 5 + [anywhere()],
        out_specs=half(x_width),
        out_shape=pltpu.HBM((rows_dev, x_width), BF),
        cost_estimate=takes(0),
        compiler_params=params(12),
        name="finish",
    )(mix, base, wide, enter_mine, enter_got, summed)
    return (attn_out, ssm_out)


def solution(mesh):
    in_specs = (
        P("seq", "head"),
        P("seq", "head"),
        P("seq", "head"),
        P("head", None),
        P("seq", "head"),
        P("seq", None, "head"),
        P(None, "head"),
        P(None, None, "head"),
        P("seq", "head"),
        P("head"),
        P("head"),
        P("seq"),
    )
    out_specs = (P(("seq", "head"), None), P("seq", "head"))
    return jax.shard_map(shards, mesh=mesh, in_specs=in_specs, out_specs=out_specs, check_vma=False)
```

```python
import functools
import math

import jax
import jax.numpy as jnp
import numpy as np
from jax import lax
from jax.experimental import pallas as pl
from jax.experimental.pallas import tpu as pltpu
from jax.sharding import PartitionSpec as P

HEAD_DIM = 128
STATE = 128
SB = 128
LEAD = 8
EDGE = 16
CHUNK = 512

NEG_BIG = -1e30
BF = jnp.bfloat16
F32 = jnp.float32
HI = lax.Precision.HIGHEST


def anywhere():
    return pl.BlockSpec(memory_space=pl.ANY)


def vmem():
    return pl.BlockSpec(memory_space=pltpu.VMEM)


def params(mebibytes):
    return pltpu.CompilerParams(vmem_limit_bytes=mebibytes << 20)


def takes(microseconds):
    return pl.CostEstimate(
        flops=int(microseconds * 1e10), bytes_accessed=int(microseconds * 3.7e6), transcendentals=0
    )


def in_hbm(x):
    return pltpu.with_memory_space_constraint(x, pltpu.HBM)


def swap(x, bit):
    count = lax.axis_size("seq")
    return lax.ppermute(x, "seq", [(i, i ^ bit) for i in range(count)])


def chip_gather(whole):
    count = lax.axis_size("seq")
    return [(0, whole)] + [(pattern, swap(whole, pattern)) for pattern in range(2, count, 2)]


def assemble(places, count, pieces, kvs, docs_ref, lead_ref):
    me = lax.axis_index("seq")
    rows = kvs.shape[0] // (2 * count)
    for piece, pattern in zip(pieces, places):
        owner = lax.bitwise_xor(me, pattern)
        back = 2 * count - 1 - owner
        kvs[pl.ds(pl.multiple_of(owner * rows, rows), rows), :] = piece[:rows]
        kvs[pl.ds(pl.multiple_of(back * rows, rows), rows), :] = piece[rows + EDGE : 2 * rows + EDGE]
        front_edge = piece[rows : rows + EDGE]
        docs_ref[pl.ds(owner, 1), :] = front_edge[:, : 2 * rows].astype(F32)[EDGE - 1 :]

        @pl.when(owner == me - 1)
        def _(front_edge=front_edge):
            lead_ref[0] = front_edge

        @pl.when(owner == me + 1)
        def _(piece=piece):
            lead_ref[1] = piece[2 * rows + EDGE :]

    own_edge = pieces[0][rows : rows + EDGE]

    @pl.when(me == 0)
    def _():
        lead_ref[0] = own_edge

    @pl.when(me == count - 1)
    def _():
        lead_ref[1] = own_edge


def attend_kernel(places, count, part, q_ref, w_ref, *rest):
    if part == 0:
        total = len(places)
        send_ref, keep_ref, kvs, docs_all, lead_ref, scores, top, acc, ctx = rest[total:]
        send_refs, keep_refs = [send_ref], [keep_ref]
        assemble(places, count, rest[:total], kvs, docs_all, lead_ref)
    else:
        kvs, docs_all = rest[:2]
        send_refs, keep_refs = rest[3:5], rest[5:7]
        scores, top, acc, ctx = rest[7:]
    me = lax.axis_index("seq")
    odd = lax.rem(lax.axis_index("head"), 2)
    rows = q_ref.shape[0] // 2
    chunk = rows // 2
    own_rows = chunk // 2
    kv_heads = kvs.shape[1] // (2 * HEAD_DIM)
    group = q_ref.shape[1] // (kv_heads * HEAD_DIM)
    tile_rows = 2 * rows
    scale = math.log2(math.e) / math.sqrt(HEAD_DIM)
    lane = lax.broadcasted_iota(jnp.int32, docs_all.shape, 1)
    is_end = lax.rem(lane, rows) == rows - 1
    k_place = lax.broadcasted_iota(jnp.int32, (chunk, tile_rows), 1)
    q_local = lax.broadcasted_iota(jnp.int32, (chunk, tile_rows), 0)
    q_local = q_local + part * own_rows + jnp.where(q_local >= own_rows, own_rows, 0)
    for side in range(2):
        block = 2 * count - 1 - me if side else me
        own = docs_all[pl.ds(lax.shift_right_logical(block, 1), 1), :]
        own = jnp.where(lax.rem(block, 2) == 1, own[:, rows:], own[:, :rows])
        own_col = jnp.transpose(jnp.broadcast_to(own, (rows, rows)))[:, :1]
        picks = [slice(c * chunk + part * own_rows, c * chunk + (part + 1) * own_rows) for c in range(2)]
        own_col = jnp.concatenate([own_col[pick] for pick in picks], axis=0)
        over = is_end & (docs_all[...] < own[:, :1])
        start = jnp.sum(over.astype(F32)).astype(jnp.int32)
        first_tile = lax.shift_right_logical(start, 1)
        last_tile = lax.shift_right_logical(block, 1) + 1
        q_place = block * rows + q_local
        heads = [list(range(kv * group, (kv + 1) * group)) for kv in range(kv_heads)]
        qs = [
            jnp.concatenate(
                [
                    q_ref[side * rows + pick.start : side * rows + pick.stop, h * HEAD_DIM : (h + 1) * HEAD_DIM]
                    for h in heads[kv]
                    for pick in picks
                ],
                axis=0,
            )
            for kv in range(kv_heads)
        ]
        top[...] = jnp.full(top.shape, NEG_BIG, F32)
        acc[...] = jnp.zeros(acc.shape, F32)

        def score_step(tile, carry, qs=qs, q_place=q_place, own_col=own_col):
            at = pl.multiple_of(tile * tile_rows, tile_rows)
            docs = docs_all[pl.ds(tile, 1), :]
            allowed = (k_place + at <= q_place) & (docs == own_col)
            for kv in range(kv_heads):
                keys = kvs[pl.ds(at, tile_rows), kv * HEAD_DIM : (kv + 1) * HEAD_DIM]
                found = lax.dot_general(
                    qs[kv], keys, (((1,), (1,)), ((), ())), preferred_element_type=F32
                )
                found = jnp.where(
                    allowed[None], found.reshape(group, chunk, tile_rows), NEG_BIG
                ).reshape(group * chunk, tile_rows)
                scores[tile, kv] = found
                top[kv] = jnp.maximum(
                    top[kv], jnp.maximum(found[:, :HEAD_DIM], found[:, HEAD_DIM:])
                )
            return carry

        lax.fori_loop(first_tile, last_tile, score_step, 0)
        row_tops = [jnp.max(top[kv], axis=1, keepdims=True) for kv in range(kv_heads)]

        def mix_step(tile, carry, row_tops=row_tops):
            at = pl.multiple_of(tile * tile_rows, tile_rows)
            for kv in range(kv_heads):
                first = (kv_heads + kv) * HEAD_DIM
                values = kvs[pl.ds(at, tile_rows), first : first + HEAD_DIM]
                values = jnp.concatenate([values, jnp.ones_like(values)], axis=1)
                weights = jnp.exp2((scores[tile, kv] - row_tops[kv]) * scale).astype(BF)
                acc[kv] += jnp.dot(weights, values, preferred_element_type=F32)
            return carry

        lax.fori_loop(first_tile, last_tile, mix_step, 0)
        for kv in range(kv_heads):
            mixed = (acc[kv, :, :HEAD_DIM] / acc[kv, :, HEAD_DIM:]).astype(BF)
            for e, h in enumerate(heads[kv]):
                ctx[side * chunk : (side + 1) * chunk, h * HEAD_DIM : (h + 1) * HEAD_DIM] = mixed[
                    e * chunk : (e + 1) * chunk
                ]
    mixed = ctx[...]
    columns = w_ref.shape[1]
    made = [
        jnp.dot(mixed, w_ref[:, at : at + 256], preferred_element_type=F32).astype(BF)
        for at in range(0, columns, 256)
    ]

    def put(low_refs, high_refs):
        wide = low_refs[0].shape[1] // 256
        for at, got in enumerate(made):
            low_ref, high_ref = low_refs[at // wide], high_refs[at // wide]
            lanes = slice(at % wide * 256, (at % wide + 1) * 256)
            for side in range(2):
                first = 2 * side * own_rows
                low_ref[side * own_rows : (side + 1) * own_rows, lanes] = got[first : first + own_rows]
                high_ref[side * own_rows : (side + 1) * own_rows, lanes] = got[
                    first + own_rows : first + 2 * own_rows
                ]

    @pl.when(odd == 0)
    def _():
        put(keep_refs, send_refs)

    @pl.when(odd == 1)
    def _():
        put(send_refs, keep_refs)


def attend(queries, out_weight, part, places, operands):
    count = lax.axis_size("seq")
    rows = queries.shape[0] // 2
    chunk = rows // 2
    kv_width = operands[0].shape[1]
    kv_heads = kv_width // (2 * HEAD_DIM)
    group = queries.shape[1] // (kv_heads * HEAD_DIM)
    columns = out_weight.shape[1]
    outs = [jax.ShapeDtypeStruct((chunk, columns), BF)] * 2
    if part == 0:
        specs = [vmem()] * len(operands)
        outs = outs + [
            pltpu.VMEM((2 * count * rows, kv_width), BF),
            pltpu.VMEM((count, 2 * rows), F32),
            pltpu.VMEM((2, EDGE, kv_width), BF),
        ]
    else:
        specs = [vmem(), vmem(), anywhere()]
        outs = [jax.ShapeDtypeStruct((chunk, columns // 2), BF)] * 4
    return pl.pallas_call(
        functools.partial(attend_kernel, places, count, part),
        in_specs=[vmem()] * 2 + specs,
        out_specs=[vmem()] * len(outs),
        out_shape=outs,
        scratch_shapes=[
            pltpu.VMEM((count, kv_heads, group * chunk, 2 * rows), F32),
            pltpu.VMEM((kv_heads, group * chunk, HEAD_DIM), F32),
            pltpu.VMEM((kv_heads, group * chunk, 2 * HEAD_DIM), F32),
            pltpu.VMEM((rows, queries.shape[1]), BF),
        ],
        compiler_params=params(8 + count * 7 // 8),
        cost_estimate=takes(8),
        name="attend_late" if part else "attend_early",
    )(queries, out_weight, *operands)


def pair_kernel(skipped, got_ref, keep_ref, after_ref, *rest):
    send_out, keep_out, *through = rest[skipped:]
    for ref in through:
        ref[...] = after_ref[...]
    own_rows = send_out.shape[0]
    low = lax.axis_index("head") < 2

    def add(first):
        rows = slice(first, first + own_rows)
        return (got_ref[rows].astype(F32) + keep_ref[rows].astype(F32)).astype(BF)

    @pl.when(low)
    def _():
        keep_out[...] = add(0)
        send_out[...] = add(own_rows)

    @pl.when(jnp.logical_not(low))
    def _():
        keep_out[...] = add(own_rows)
        send_out[...] = add(0)


def pair_sum(got, keep, after, through, *also):
    rows, columns = keep.shape
    outs = [jax.ShapeDtypeStruct((rows // 2, columns), BF)] * 2
    if through:
        outs = outs + [jax.ShapeDtypeStruct(after.shape, after.dtype)]
    return pl.pallas_call(
        functools.partial(pair_kernel, len(also)),
        in_specs=[vmem(), vmem(), vmem() if through else anywhere()] + [anywhere()] * len(also),
        out_specs=[vmem()] * len(outs),
        out_shape=outs,
        compiler_params=params(8),
        cost_estimate=takes(0),
        name="pair_sum",
    )(got, keep, after, *also)


def last_kernel(early_got, early_keep, got_a, keep_a, got_b, keep_b, after_ref, out_ref, done_ref):
    done_ref[...] = jnp.zeros(done_ref.shape, F32)
    rows, columns = early_got.shape
    out_ref[:rows] = (early_got[...].astype(F32) + early_keep[...].astype(F32)).astype(BF)
    for at, (got, keep) in enumerate(((got_a, keep_a), (got_b, keep_b))):
        lanes = slice(at * columns // 2, (at + 1) * columns // 2)
        out_ref[rows:, lanes] = (got[...].astype(F32) + keep[...].astype(F32)).astype(BF)


def prepare_kernel(k_ref, v_ref, docs_ref, xf_ref, xb_ref, bf_ref, bb_ref, kv_ref):
    rows = k_ref.shape[0] // 2
    width = k_ref.shape[1]
    docs = jnp.broadcast_to(docs_ref[...], (LEAD, 2 * rows)).astype(F32)[:1]
    docs = jnp.concatenate([docs, jnp.zeros((1, 2 * width - 2 * rows), F32)], axis=1)
    for half, x_ref, bc_ref in ((0, xf_ref, bf_ref), (1, xb_ref, bb_ref)):
        first = half * (rows + EDGE)
        kv_ref[first : first + rows, :width] = k_ref[half * rows : (half + 1) * rows]
        kv_ref[first : first + rows, width:] = v_ref[half * rows : (half + 1) * rows]
        x_edge = x_ref[...].astype(F32)
        bc_edge = jnp.concatenate([bc_ref[:, 0, :], bc_ref[:, 1, :]], axis=1).astype(F32)
        lines = []
        for t in range(LEAD - 3, LEAD):
            for edge in (x_edge, bc_edge):
                lines += [edge[t : t + 1, c : c + CHUNK] for c in range(0, edge.shape[1], CHUNK)]
        kv_ref[first + rows : first + rows + EDGE] = jnp.concatenate(lines + [docs], axis=0).astype(BF)


def load_kernel(w_ref, q_ref, x_ref, bc_ref, kv_ref, w_out, q_out, x_out, bc_out, kv_out, bc_in, sems):
    bc_copy = pltpu.make_async_copy(bc_ref, bc_in, sems.at[6])
    bc_copy.start()
    copies = [
        pltpu.make_async_copy(q_ref, q_out, sems.at[0]),
        pltpu.make_async_copy(x_ref, x_out, sems.at[5]),
    ]
    parts = 4
    size = w_ref.shape[0] // parts
    for at in range(parts):
        piece = pl.ds(at * size, size)
        copies.append(pltpu.make_async_copy(w_ref.at[piece], w_out.at[piece], sems.at[at + 1]))
    for copy in copies:
        copy.start()
    kv_out[...] = kv_ref[...]
    bc_copy.wait()
    part = bc_in.shape[2]
    for at in range(2):
        bc_out[:, at * part : (at + 1) * part] = bc_in[:, at, :]
    for copy in copies:
        copy.wait()


def spread(values, expand):
    high = values.astype(BF)
    low = (values - high.astype(F32)).astype(BF)
    return jnp.dot(jnp.concatenate([high, low], axis=1), expand, preferred_element_type=F32)


def local_kernel(
    count, docs_ref, lead_ref, x_ref, bc_ref, tx_ref, tbc_ref, step_ref, rate_ref, expand_ref, after_ref,
    xc_ref, xt_ref, mix_ref, reach_ref, keep_ref, send_ref, ext,
):
    half = pl.program_id(0)
    me = lax.axis_index("seq")
    core = lax.rem(me, 2)
    rows = xc_ref.shape[0]
    x_width = x_ref.shape[1]
    mine = pl.ds(pl.multiple_of(half * rows, rows), rows)
    bc_width = bc_ref.shape[1]
    groups = bc_width // (2 * STATE)
    x_group = x_width // groups
    block = jnp.where(half == 0, me, 2 * count - 1 - me)

    def doc_row(where):
        got = docs_ref[pl.ds(lax.shift_right_logical(where, 1), 1), :]
        return jnp.where(lax.rem(where, 2) == 1, got[:, rows:], got[:, :rows])

    own = doc_row(block)
    before = jnp.where(block > 0, doc_row(jnp.maximum(block - 1, 0)), -1.0)
    lead = lead_ref[half].astype(F32)
    chunks = (x_width + bc_width) // CHUNK
    lane = lax.broadcasted_iota(jnp.int32, (1, rows), 1)
    own_b = jnp.broadcast_to(own, (8, rows))
    before_b = jnp.broadcast_to(before, (8, rows))
    lane_b = jnp.broadcast_to(lane, (8, rows))
    lines = []
    for k in range(1, 4):
        moved = jnp.where(lane_b < k, pltpu.roll(before_b, k, 1), pltpu.roll(own_b, k, 1))
        lines.append((moved == own_b)[:1].astype(F32))
    last_doc = before[:, rows - 1 :]
    end_doc = own[:, rows - 1 :]
    lines.append((own == end_doc).astype(F32))
    lines.append((own == last_doc).astype(F32))
    lines.append(own)
    lines.append(jnp.zeros((2, rows), F32))
    table = jnp.transpose(jnp.concatenate(lines, axis=0))
    same = [table[:, k : k + 1] for k in range(3)]
    ending, alive, own_col = table[:, 3:4], table[:, 4:5], table[:, 5:6]

    def conv(source, taps, chunk, width):
        for t in range(3):
            for c in range(width // CHUNK):
                line = t * chunks + chunk + c
                ext[LEAD - 3 + t : LEAD - 2 + t, c * CHUNK : (c + 1) * CHUNK] = lead[line : line + 1]
        ext[LEAD:, :width] = source.astype(F32)
        total = ext[LEAD:, :width] * taps[0:1]
        for k in range(1, 4):
            total += same[k - 1] * (ext[LEAD - k : LEAD - k + rows, :width] * taps[k : k + 1])
        return (total * (0.5 * jnp.tanh(0.5 * total) + 0.5)).astype(BF)

    tbc = jnp.concatenate([tbc_ref[:, 0, :], tbc_ref[:, 1, :]], axis=1)
    bc = conv(bc_ref[mine, :], tbc, x_width // CHUNK, bc_width)
    row_id = lax.broadcasted_iota(jnp.int32, (rows, rows), 0)
    col_id = lax.broadcasted_iota(jnp.int32, (rows, rows), 1)
    lower = row_id >= col_id
    steps = jnp.transpose(step_ref[...])
    logs = jnp.dot(
        lower.astype(F32), -rate_ref[...] * steps, preferred_element_type=F32, precision=HI
    )
    grow = jnp.exp(-logs) * steps
    reach = jnp.exp(logs)
    reach_ref[...] = reach
    expand = expand_ref[...]
    fade_end = spread(reach[rows - 8 :], expand)[7:8]
    carries = jnp.max(jnp.where(end_doc == last_doc, 1.0, 0.0))
    fade = fade_end * carries
    allowed = lower & (own_col == own)
    for g in range(groups):
        lanes = slice(g * x_group, (g + 1) * x_group)
        xc = conv(x_ref[mine, lanes], tx_ref[:, lanes], g * x_group // CHUNK, x_group)
        xc_ref[:, lanes] = xc
        xt = (xc.astype(F32) * spread(grow, expand[:, lanes])).astype(BF)
        xt_ref[:, lanes] = xt
        b = bc[:, g * STATE : (g + 1) * STATE]
        c = bc[:, (groups + g) * STATE : (groups + g + 1) * STATE]
        cb = lax.dot_general(c, b, (((1,), (1,)), ((), ())), preferred_element_type=F32)
        mix_ref[:, g * 2 * rows : g * 2 * rows + rows] = jnp.where(allowed, cb, 0.0).astype(BF)
        mix_ref[:, g * 2 * rows + rows : (g + 1) * 2 * rows] = (c.astype(F32) * alive).astype(BF)
        b_t = jnp.transpose(b.astype(F32) * ending).astype(BF)
        state = jnp.dot(b_t, xt, preferred_element_type=F32) * fade_end[:, lanes]
        state = state.astype(BF)
        tail = fade_rows(fade[:, lanes])

        @pl.when(core == g)
        def _(state=state, tail=tail):
            keep_ref[0, :STATE] = state
            keep_ref[0, STATE:] = tail

        @pl.when(core != g)
        def _(state=state, tail=tail):
            send_ref[0, :STATE] = state
            send_ref[0, STATE:] = tail


def unpack(packed):
    state = packed[:STATE].astype(F32)
    tail = packed[STATE : STATE + LEAD].astype(F32)
    return tail[:1] + tail[LEAD - 1 :], state


def fade_rows(fade):
    high = fade.astype(BF).astype(F32)
    shape = (LEAD // 2, fade.shape[1])
    parts = [jnp.broadcast_to(high, shape), jnp.broadcast_to(fade - high, shape)]
    return jnp.concatenate(parts, axis=0).astype(BF)


def join_kernel(mine_ref, other_ref, after_ref, out_ref):
    core = lax.rem(lax.axis_index("seq"), 2)
    for half in range(2):
        first_is_mine = core == half

        def joined(first, second, half=half):
            fade_a, state_a = unpack(first)
            fade_b, state_b = unpack(second)
            out_ref[half, :STATE] = (fade_b * state_a + state_b).astype(BF)
            out_ref[half, STATE:] = fade_rows(fade_a * fade_b)

        @pl.when(first_is_mine)
        def _(half=half):
            joined(mine_ref[half], other_ref[half])

        @pl.when(jnp.logical_not(first_is_mine))
        def _(half=half):
            joined(other_ref[half], mine_ref[half])


def enter_kernel(places, count, mine_ref, other_ref, after_ref, also_ref, *rest):
    total = len(places)
    pieces = rest[:total]
    keep_ref, send_ref, fronts, backs, sems, run = rest[total:]
    me = lax.axis_index("seq")
    core = lax.rem(me, 2)
    chip = lax.shift_right_logical(me, 1)
    chips = count // 2
    copies = []
    for at, pattern in enumerate(places):
        slot = lax.bitwise_xor(chip, pattern // 2)
        for half, target in enumerate((fronts, backs)):
            copy = pltpu.make_async_copy(pieces[at].at[half], target.at[slot], sems.at[len(copies)])
            copy.start()
            copies.append(copy)
    for copy in copies:
        copy.wait()
    run[...] = jnp.zeros(run.shape, F32)

    def put(half):
        entering = run[...]
        mine_first = core == half

        def after(packed):
            fade, state = unpack(packed)
            return (fade * entering + state).astype(BF)

        @pl.when(mine_first)
        def _():
            keep_ref[half] = entering.astype(BF)
            send_ref[half] = after(mine_ref[half])

        @pl.when(jnp.logical_not(mine_first))
        def _():
            send_ref[half] = entering.astype(BF)
            keep_ref[half] = after(other_ref[half])

    def front_step(at, carry):
        @pl.when(at == chip)
        def _():
            put(0)

        fade, state = unpack(fronts[at])
        run[...] = fade * run[...] + state
        return carry

    lax.fori_loop(0, chips, front_step, 0)

    def back_step(k, carry):
        at = chips - 1 - k

        @pl.when(at == chip)
        def _():
            put(1)

        fade, state = unpack(backs[at])
        run[...] = fade * run[...] + state
        return carry

    lax.fori_loop(0, chips - chip, back_step, 0)


def ready_kernel(xc_ref, xt_ref, mix_ref, reach_ref, skip_ref, expand_ref, base_ref, wide_ref):
    rows = mix_ref.shape[0] // 2
    x_width = xc_ref.shape[1]
    groups = mix_ref.shape[1] // (2 * rows)
    x_group = x_width // groups
    skip = spread(jnp.broadcast_to(skip_ref[...], (8, skip_ref.shape[1])), expand_ref[...])[:1]
    for half in range(2):
        mine = slice(half * rows, (half + 1) * rows)
        for g in range(groups):
            lanes = slice(g * x_group, (g + 1) * x_group)
            mix = mix_ref[mine, g * 2 * rows : g * 2 * rows + rows]
            made = jnp.dot(mix, xt_ref[mine, lanes], preferred_element_type=F32)
            wide = spread(reach_ref[mine, :], expand_ref[:, lanes])
            wide_ref[mine, lanes] = wide
            base_ref[mine, lanes] = made * wide + skip[:, lanes] * xc_ref[mine, lanes].astype(F32)


def finish_kernel(mix_ref, base_ref, wide_ref, mine_ref, other_ref, after_ref, out_ref):
    core = lax.rem(lax.axis_index("seq"), 2)
    half = pl.program_id(0)
    rows, x_width = out_ref.shape
    mine = pl.ds(pl.multiple_of(half * rows, rows), rows)
    groups = mix_ref.shape[1] // (2 * rows)
    x_group = x_width // groups
    for g in range(groups):
        lanes = slice(g * x_group, (g + 1) * x_group)
        reads = mix_ref[mine, g * 2 * rows + rows : (g + 1) * 2 * rows]

        def put(state, reads=reads, lanes=lanes):
            made = jnp.dot(reads, state, preferred_element_type=F32)
            out_ref[:, lanes] = (base_ref[mine, lanes] + wide_ref[mine, lanes] * made).astype(BF)

        @pl.when(core == g)
        def _(put=put):
            put(mine_ref[half])

        @pl.when(core != g)
        def _(put=put):
            put(other_ref[half])


def shards(
    queries, key_rows, value_rows, out_weight, ssm_input, bc_input, conv_input, conv_bc, step_size,
    decay_rate, skip_gain, doc_ids,
):
    count = lax.axis_size("seq")
    rows_dev = queries.shape[0]
    rows = rows_dev // 2
    x_width = ssm_input.shape[1]
    bc_width = bc_input.shape[1] * bc_input.shape[2]
    taps = conv_input.shape[0]
    groups = bc_width // (2 * STATE)
    heads = decay_rate.shape[0]
    x_group = x_width // groups

    docs = doc_ids.reshape(1, rows_dev)
    row_block = rows // LEAD
    kv = pl.pallas_call(
        prepare_kernel,
        grid=(1,),
        in_specs=[
            vmem(),
            vmem(),
            vmem(),
            pl.BlockSpec((LEAD, x_width), lambda t: (row_block - 1, 0)),
            pl.BlockSpec((LEAD, x_width), lambda t: (2 * row_block - 1, 0)),
            pl.BlockSpec((LEAD,) + bc_input.shape[1:], lambda t: (row_block - 1, 0, 0)),
            pl.BlockSpec((LEAD,) + bc_input.shape[1:], lambda t: (2 * row_block - 1, 0, 0)),
        ],
        out_specs=vmem(),
        out_shape=jax.ShapeDtypeStruct((rows_dev + 2 * EDGE, 2 * key_rows.shape[1]), BF),
        compiler_params=params(12),
        name="prepare",
    )(
        in_hbm(key_rows), in_hbm(value_rows), in_hbm(docs), in_hbm(ssm_input), in_hbm(ssm_input),
        in_hbm(bc_input), in_hbm(bc_input),
    )

    weight, query_rows, x_rows, bc, kv_again = pl.pallas_call(
        load_kernel,
        in_specs=[anywhere()] * 4 + [vmem()],
        out_specs=[vmem()] * 5,
        out_shape=[
            pltpu.VMEM(out_weight.shape, BF),
            pltpu.VMEM(queries.shape, BF),
            pltpu.VMEM(ssm_input.shape, BF),
            pltpu.VMEM((rows_dev, bc_width), BF),
            jax.ShapeDtypeStruct(kv.shape, BF),
        ],
        scratch_shapes=[pltpu.VMEM(bc_input.shape, BF), pltpu.SemaphoreType.DMA((7,))],
        compiler_params=params(10),
        cost_estimate=takes(5),
        name="load",
    )(in_hbm(out_weight), in_hbm(queries), in_hbm(ssm_input), in_hbm(bc_input), kv)

    pieces = chip_gather(kv)
    pieces = pieces + [(1, swap(kv_again, 1))] + [(pattern ^ 1, swap(array, 1)) for pattern, array in pieces[1:]]

    expand = np.repeat(np.eye(heads, dtype=np.float32), x_width // heads, axis=1)
    expand = jnp.asarray(np.concatenate([expand, expand], axis=0), BF)
    pack_rows = STATE + LEAD
    full = lambda shape: pl.BlockSpec(shape, lambda h: (0,) * len(shape))
    half = lambda width: pl.BlockSpec((rows, width), lambda h: (h, 0))
    packed_spec = pl.BlockSpec((1, pack_rows, x_group), lambda h: (h, 0, 0))
    pair = [(i, i ^ 1) for i in range(4)]
    cross = [(i, i ^ 2) for i in range(4)]
    early_send, early_keep, kvs, docs_all, lead = attend(
        query_rows, weight, 0, [pattern for pattern, _ in pieces], [array for _, array in pieces]
    )
    early_pair = lax.ppermute(early_send, "head", pair)
    late = attend(query_rows, weight, 1, None, [kvs, docs_all, early_keep])
    late_keep = late[2]
    late_pairs = [lax.ppermute(send, "head", pair) for send in late[:2]]
    xc, xt, mix, reach, keep, send = pl.pallas_call(
        functools.partial(local_kernel, count),
        grid=(2,),
        in_specs=[
            vmem(),
            vmem(),
            vmem(),
            vmem(),
            full((taps, x_width)),
            full(conv_bc.shape),
            pl.BlockSpec((heads, rows), lambda h: (0, h)),
            full((1, heads)),
            full((2 * heads, x_width)),
            anywhere(),
        ],
        out_specs=[half(x_width), half(x_width), half(groups * 2 * rows), half(heads), packed_spec, packed_spec],
        out_shape=[
            pltpu.HBM((rows_dev, x_width), BF),
            pltpu.HBM((rows_dev, x_width), BF),
            pltpu.HBM((rows_dev, groups * 2 * rows), BF),
            pltpu.HBM((rows_dev, heads), F32),
            jax.ShapeDtypeStruct((2, pack_rows, x_group), BF),
            jax.ShapeDtypeStruct((2, pack_rows, x_group), BF),
        ],
        scratch_shapes=[pltpu.VMEM((rows + LEAD, x_group), F32)],
        cost_estimate=takes(5.5),
        compiler_params=params(16 + count // 4),
        name="local_states",
    )(
        docs_all, lead, x_rows, bc, in_hbm(conv_input), in_hbm(conv_bc), in_hbm(step_size.T),
        decay_rate.reshape(1, heads), expand, late_keep,
    )

    early_cross, early_mine, send = pair_sum(early_pair, early_keep, send, True)
    other = swap(send, 1)
    early_got = lax.ppermute(early_cross, "head", cross)
    chip = pl.pallas_call(
        join_kernel,
        in_specs=[vmem(), vmem(), anywhere()],
        out_specs=vmem(),
        out_shape=jax.ShapeDtypeStruct(keep.shape, BF),
        compiler_params=params(12),
        cost_estimate=takes(0),
        name="join_states",
    )(keep, other, late_keep)
    base, wide = pl.pallas_call(
        ready_kernel,
        in_specs=[vmem()] * 6,
        out_specs=[vmem()] * 2,
        out_shape=[pltpu.VMEM((rows_dev, x_width), F32)] * 2,
        cost_estimate=takes(4),
        compiler_params=params(12),
        name="ready",
    )(xc, xt, mix, reach, skip_gain.reshape(1, heads), expand)
    late_cross, late_mine = pair_sum(late_pairs[0], late[2], late[2], False, base)
    late_got = [lax.ppermute(late_cross, "head", cross)]
    late_mine = [late_mine]
    late_cross, mine = pair_sum(late_pairs[1], late[3], early_got, False)
    late_got.append(lax.ppermute(late_cross, "head", cross))
    late_mine.append(mine)
    chip_pieces = chip_gather(chip)
    chips = count // 2
    state_shape = jax.ShapeDtypeStruct((2, STATE, x_group), BF)
    enter_mine, enter_other = pl.pallas_call(
        functools.partial(enter_kernel, [pattern for pattern, _ in chip_pieces], count),
        in_specs=[vmem(), vmem()] + [anywhere()] * (2 + len(chip_pieces)),
        out_specs=[vmem(), vmem()],
        out_shape=[state_shape, state_shape],
        scratch_shapes=[
            pltpu.VMEM((chips, pack_rows, x_group), BF),
            pltpu.VMEM((chips, pack_rows, x_group), BF),
            pltpu.SemaphoreType.DMA((2 * chips,)),
            pltpu.VMEM((STATE, x_group), F32),
        ],
        compiler_params=params(14 + chips),
        cost_estimate=takes(0),
        name="enter_states",
    )(keep, other, *late_got, *[array for _, array in chip_pieces])
    enter_got = swap(enter_other, 1)

    attn_out, summed = pl.pallas_call(
        last_kernel,
        in_specs=[vmem()] * 6 + [anywhere()],
        out_specs=[vmem()] * 2,
        out_shape=[
            jax.ShapeDtypeStruct((rows // 2, out_weight.shape[1]), BF),
            jax.ShapeDtypeStruct((8, 128), F32),
        ],
        compiler_params=params(6),
        cost_estimate=takes(0),
        name="last_sum",
    )(early_got, early_mine, late_got[0], late_mine[0], late_got[1], late_mine[1], enter_other)
    ssm_out = pl.pallas_call(
        finish_kernel,
        grid=(2,),
        in_specs=[vmem()] * 5 + [anywhere()],
        out_specs=half(x_width),
        out_shape=pltpu.HBM((rows_dev, x_width), BF),
        cost_estimate=takes(0),
        compiler_params=params(12),
        name="finish",
    )(mix, base, wide, enter_mine, enter_got, summed)
    return (attn_out, ssm_out)


def solution(mesh):
    in_specs = (
        P("seq", "head"),
        P("seq", "head"),
        P("seq", "head"),
        P("head", None),
        P("seq", "head"),
        P("seq", None, "head"),
        P(None, "head"),
        P(None, None, "head"),
        P("seq", "head"),
        P("head"),
        P("head"),
        P("seq"),
    )
    out_specs = (P(("seq", "head"), None), P("seq", "head"))
    return jax.shard_map(shards, mesh=mesh, in_specs=in_specs, out_specs=out_specs, check_vma=False)
```
